512 devices in a mesh: eb: 64 (over y, z), col: 8 (over x, core).
Axes of the slice: x: 4, y: 4, z: 16, core: 2. Of those that a mesh axis runs over, the one named last changes fastest.
Arguments:
- g_lesser: float32 [8, 768, 64, 2, 256], P('col', 'eb'), may hold values from -6 to 6
- g_greater: float32 [8, 768, 64, 2, 256], P('col', 'eb'), may hold values from -6 to 6
- owner_tiles: int32 [8, 768], P('col', 'eb'), may hold values from 0 to 512, as said below
- energy_map: int32 [64], replicated, may hold values from 0 to 63, each once
- coulomb: float32 [8, 2, 256, 256], P('col'), may hold values from -0.21875 to 0.21875
Outputs:
- screened: float32 [64, 8, 2, 2, 256, 256], P('eb', 'col')
The draws below stay inside these ranges and needn't reach their ends.
Inputs may be any that keep to these rules, and one draw needn't show every extreme that they name: `owner_tiles`: row c lists the tiles of column group c held by each index of eb in 12 consecutive slots; every tile 0 to 511 appears exactly once in the row, 512 marks an empty slot, and in every draw some index of eb holds exactly 12 tiles. `energy_map`: each energy appears exactly once.
All inputs are finite; a program needn't handle non-finite values.
Results may differ from the reference program's by a relative error of at most 0.00007.
Values sent between devices are 32-bit elements; how exact they have to be, the bound alone decides.
No kernel may reach another device: no remote copies, remote signals or barrier semaphores. Data moves between devices by JAX's collectives and lax.ppermute only.
A program may use at most 64 MiB of HBM per device.

```python
import math
import jax
import jax.numpy as jnp
from jax import lax

B = 256
CB = 1
NB = 8
NE = 64
TILES = 512
TCAP = 12
SLOTS = 768
N_EB = 64
N_COL = 8


def draw_owner_tiles(key, part):
    average = TILES // N_EB
    halfway = average // 2
    pairs = N_EB // 2

    def one_group(group_key):
        key_shift, key_order, key_tiles, key_slots = jax.random.split(group_key, 4)
        shifts = jax.random.randint(key_shift, (pairs,), 0, halfway + 1).astype(jnp.int32)
        shifts = shifts.at[0].set(halfway)
        device_order = jax.random.permutation(key_order, N_EB)
        counts = jnp.zeros((N_EB,), jnp.int32)
        counts = counts.at[device_order[:pairs]].set(average + shifts)
        counts = counts.at[device_order[pairs:]].set(average - shifts)
        starts = jnp.cumsum(counts) - counts
        tile_order = jax.random.permutation(key_tiles, TILES).astype(jnp.int32)
        position = jnp.arange(TCAP, dtype=jnp.int32)
        scores = jax.random.randint(key_slots, (N_EB, TCAP), 0, 1 << 20).astype(jnp.int32) * TCAP + position[None, :]
        slot_order = jnp.argsort(scores, axis=1).astype(jnp.int32)
        live = slot_order < counts[:, None]
        source = jnp.clip(starts[:, None] + slot_order, 0, TILES - 1)
        listed = jnp.where(live, tile_order[source], TILES)
        return listed.reshape(-1).astype(jnp.int32)
    group_keys = jax.random.split(key, N_COL)
    return jax.vmap(one_group)(group_keys)


def levels(own_key, extent, cuts, low, largest):
    factor_of, own = 1.0, jax.random.fold_in(own_key, 6)
    for axis_at, blocks in cuts:
        steps = jnp.exp(jax.random.uniform(jax.random.fold_in(own, axis_at), (blocks,), jnp.float32, low / len(cuts), largest / len(cuts)))
        factor_of = factor_of * jnp.repeat(steps, extent[axis_at] // blocks).reshape([-1 if axis == axis_at else 1 for axis in range(len(extent))])
    return factor_of


def scatter_about(stream_key, dims, spread, most, cuts=(), kind=jnp.bfloat16):
    values = spread * jax.random.normal(stream_key, dims, jnp.float32)
    if cuts:
        values = values * levels(stream_key, dims, cuts, -0.22, 0.18)
    return jnp.clip(values, -most, most).astype(kind)


def setup_inputs(seed: int = 0) -> dict:
    arg_keys = jax.random.split(jax.random.key(seed), 6)
    g_lesser = scatter_about(arg_keys[0], (N_COL, SLOTS, NE, 2, B), 1.0, 6.0, ((0, 8), (1, 64)), jnp.float32)
    g_greater = scatter_about(arg_keys[1], (N_COL, SLOTS, NE, 2, B), 1.0, 6.0, ((0, 8), (1, 64)), jnp.float32)
    owner_tiles = draw_owner_tiles(jax.random.fold_in(arg_keys[5], 71), 0)
    energy_map = jax.random.permutation(arg_keys[3], NE).astype(jnp.int32)
    coulomb = scatter_about(arg_keys[4], (NB, 2, B, B), (3 * B) ** -0.5, 0.21875, ((0, 8),), jnp.float32)
    return {"g_lesser": g_lesser, "g_greater": g_greater, "owner_tiles": owner_tiles, "energy_map": energy_map, "coulomb": coulomb}


precise = lax.Precision.HIGHEST

def left_product(coupling, blocks):
    return jnp.einsum('cab,ecrbd->ecrad', coupling, blocks, precision=precise)

def left_transposed(coupling, blocks):
    return jnp.einsum('cba,ecrbd->ecrad', coupling, blocks, precision=precise)

def right_product(blocks, coupling):
    return jnp.einsum('ecrab,cbd->ecrad', blocks, coupling, precision=precise)

def right_transposed(blocks, coupling):
    return jnp.einsum('ecrab,cdb->ecrad', blocks, coupling, precision=precise)

def upper_blocks(lower):
    flipped = jnp.swapaxes(lower, -1, -2)
    return jnp.stack([-flipped[:, :, 0], flipped[:, :, 1]], axis=2)

def screened_columns(diag_prev, lower_prev, diag_here, lower_here, diag_next, lower_next, vl_prev, vd_here, vl_here, vd_next, vl_next):
    upper_prev = upper_blocks(lower_prev)
    upper_here = upper_blocks(lower_here)
    z_above = right_transposed(diag_prev, vl_prev) + right_transposed(upper_prev, vd_here)
    z_middle = right_transposed(lower_prev, vl_prev) + right_transposed(diag_here, vd_here) + right_product(upper_here, vl_here)
    z_below = right_transposed(lower_here, vd_here) + right_product(diag_next, vl_here)
    z_farther = right_product(lower_next, vl_here)
    y_diag = left_product(vl_prev, z_above) + left_product(vd_here, z_middle) + left_transposed(vl_here, z_below)
    y_lower = left_product(vl_here, z_middle) + left_product(vd_next, z_below) + left_transposed(vl_next, z_farther)
    return jnp.stack([y_diag, y_lower], axis=2)

def correlate(lesser, greater):
    n_energy = lesser.shape[0]
    wave_less = lesser[:, 0] + 1j * lesser[:, 1]
    wave_more = greater[:, 0] + 1j * greater[:, 1]
    spec_less = jnp.fft.fft(wave_less, n=2 * n_energy, axis=0)
    spec_more = jnp.fft.fft(wave_more, n=2 * n_energy, axis=0)
    series = jnp.fft.ifft(spec_less * jnp.conj(spec_more), axis=0)[:n_energy] / math.sqrt(n_energy)
    return jnp.stack([jnp.imag(series), -jnp.real(series)], axis=1).astype(jnp.float32)

def reference(g_lesser, g_greater, owner_tiles, energy_map, coulomb):

    def column_group(item):
        lesser, greater, tile_ids = item
        dense_less = jnp.zeros((TILES + 1, NE, 2, B), jnp.float32).at[tile_ids].set(lesser)[:TILES]
        dense_more = jnp.zeros((TILES + 1, NE, 2, B), jnp.float32).at[tile_ids].set(greater)[:TILES]
        flat_less = dense_less.transpose(1, 2, 0, 3).reshape(NE, 2, TILES * B)
        flat_more = dense_more.transpose(1, 2, 0, 3).reshape(NE, 2, TILES * B)
        polar = correlate(flat_less, flat_more)
        return polar.reshape(NE, 2, CB, 2, B, B).transpose(0, 2, 3, 1, 4, 5)
    groups = lax.map(column_group, (g_lesser, g_greater, owner_tiles))
    polar_all = jnp.swapaxes(groups, 0, 1).reshape(NE, NB, 2, 2, B, B)
    ordered = jnp.take(polar_all, energy_map, axis=0)
    vd_here = coulomb[:, 0]
    vl_here = coulomb[:, 1]
    vl_prev = jnp.roll(vl_here, 1, axis=0)
    vd_next = jnp.roll(vd_here, -1, axis=0)
    vl_next = jnp.roll(vl_here, -1, axis=0)

    def one_energy(blocks):
        diag_here = blocks[None, :, 0]
        lower_here = blocks[None, :, 1]
        result = screened_columns(jnp.roll(diag_here, 1, axis=1), jnp.roll(lower_here, 1, axis=1), diag_here, lower_here, jnp.roll(diag_here, -1, axis=1), jnp.roll(lower_here, -1, axis=1), vl_prev, vd_here, vl_here, vd_next, vl_next)
        return result[0]
    return lax.map(one_energy, ordered)
```

```python
import math

import jax
import jax.numpy as jnp
import numpy as np
from jax import lax
from jax.experimental import pallas as pl
from jax.experimental.pallas import tpu as pltpu
from jax.sharding import PartitionSpec as P

f32 = jnp.float32
bf16 = jnp.bfloat16
LANES = 128


def halves(x):
    high = x.astype(bf16)
    low = (x - high.astype(f32)).astype(bf16)
    return high, low


def product(a, b):
    (ah, al), (bh, bl) = a, b
    dot = lambda u, v: jnp.dot(u, v, preferred_element_type=f32)
    return dot(ah, bh) + (dot(ah, bl) + dot(al, bh))


def transform_tables(n_energy):
    padded = 2 * n_energy
    k = np.arange(padded)
    n = np.arange(n_energy)
    angle = 2.0 * np.pi * (np.outer(k, n) % padded) / padded
    c, s = np.cos(angle), np.sin(angle)
    forward = np.block([[c, s], [-s, c]])
    scale = 1.0 / (padded * math.sqrt(n_energy))
    backward = np.block([[s.T, c.T], [-c.T, s.T]]) * scale
    return forward.astype(np.float32), backward.astype(np.float32)


def numpy_halves(x):
    high = x.astype(bf16)
    low = (x - high.astype(np.float32)).astype(bf16)
    return high, low


def correlate_kernel(
    slots, step_slots, n_energy, n_dest, stride,
    tiles_ref, emap_ref, fh_ref, fl_ref, bh_ref, bl_ref, less_ref, more_ref,
    out_ref, backh, backl,
):
    step = pl.program_id(0)

    @pl.when(step == 0)
    def _():
        row = jnp.broadcast_to(emap_ref[...], (n_dest, n_energy))
        i0 = lax.broadcasted_iota(jnp.int32, (n_dest, n_energy), 0)
        i1 = lax.broadcasted_iota(jnp.int32, (n_dest, n_energy), 1)
        column = jnp.sum(jnp.where(i0 == i1, row, 0), axis=1, keepdims=True)
        pick = jnp.where(i1 == column, 1.0, 0.0).astype(bf16)
        for part in range(2):
            rows = slice(part * n_energy, (part + 1) * n_energy)
            dest = slice(part * n_dest, (part + 1) * n_dest)
            for source, target in ((bh_ref, backh), (bl_ref, backl)):
                target[dest, :] = jnp.dot(
                    pick, source[rows, :], preferred_element_type=f32
                ).astype(bf16)
        lane = lax.broadcasted_iota(jnp.int32, (1, LANES), 1)
        ids = jnp.zeros((1, LANES), jnp.int32)
        for s in range(slots):
            ids = jnp.where(lane == s, tiles_ref[0, s], ids)
        out_ref[pl.ds(stride - 1, n_dest, stride=stride), :] = jnp.broadcast_to(
            ids.astype(f32), (n_dest, LANES)
        )

    forward = (fh_ref[...], fl_ref[...])
    backward = (backh[...], backl[...])

    def spectrum(ref, i):
        piece = lambda q: ref[i, pl.ds(q, n_energy, stride=4), :]
        re = jnp.concatenate([piece(0), piece(2)], axis=1)
        im = jnp.concatenate([piece(1), piece(3)], axis=1)
        return product(forward, halves(jnp.concatenate([re, im], axis=0)))

    for i in range(step_slots):
        less = spectrum(less_ref, i)
        more = spectrum(more_ref, i)
        half = 2 * n_energy
        lr, li, mr, mi = less[:half], less[half:], more[:half], more[half:]
        cross = jnp.concatenate([lr * mr + li * mi, li * mr - lr * mi], axis=0)
        series = product(backward, halves(cross))
        slot = step * step_slots + i
        for q in range(4):
            value = series[(q // 2) * n_dest:(q // 2 + 1) * n_dest,
                           (q % 2) * LANES:(q % 2 + 1) * LANES]
            out_ref[pl.ds(slot * 4 + q, n_dest, stride=stride), :] = value


def correlate(less, more, tiles, emap, n_dest, interpret=False):
    slots, n_energy = less.shape[0], less.shape[1]
    stride = slots * 4 + 1
    step_slots = 2
    forward, backward = transform_tables(n_energy)
    tables = numpy_halves(forward) + numpy_halves(backward)

    def packed(x):
        x = x.reshape(slots, n_energy, 2, 2, LANES).transpose(0, 1, 3, 2, 4)
        return x.reshape(slots, n_energy * 4, LANES)

    whole = lambda shape: pl.BlockSpec(shape, lambda i: (0,) * len(shape))
    slot_block = pl.BlockSpec((step_slots, n_energy * 4, LANES), lambda i: (i, 0, 0))
    kernel = lambda *refs: correlate_kernel(
        slots, step_slots, n_energy, n_dest, stride, *refs
    )
    return pl.pallas_call(
        kernel,
        grid=(slots // step_slots,),
        in_specs=[
            pl.BlockSpec(memory_space=pltpu.SMEM),
            whole((1, n_energy)),
            whole(tables[0].shape), whole(tables[1].shape),
            whole(tables[2].shape), whole(tables[3].shape),
            slot_block, slot_block,
        ],
        out_specs=whole((n_dest * stride, LANES)),
        out_shape=jax.ShapeDtypeStruct((n_dest * stride, LANES), f32),
        scratch_shapes=[
            pltpu.VMEM((2 * n_dest, 4 * n_energy), bf16),
            pltpu.VMEM((2 * n_dest, 4 * n_energy), bf16),
        ],
        interpret=interpret,
    )(tiles, emap.reshape(1, n_energy), *[jnp.asarray(t) for t in tables],
      packed(less), packed(more))


def place_kernel(slots, n_source, order, group, in_ref, out_ref):
    stride = slots * 4 + 1
    ids = in_ref[pl.ds(stride - 1, n_source, stride=stride), :]
    by_slot = jnp.transpose(ids)
    total_h = total_l = None
    for g in range(0, slots, group):
        row = jnp.concatenate([by_slot[s:s + 1, :] for s in range(g, g + group)], axis=1)
        width = group * n_source
        tile = lax.broadcasted_iota(jnp.int32, (2 * order, width), 0).astype(f32)
        pick = jnp.where(tile == row, 1.0, 0.0).astype(bf16)
        values = jnp.concatenate(
            [
                jnp.concatenate(
                    [in_ref[pl.ds(s * 4 + q, n_source, stride=stride), :] for q in range(4)],
                    axis=1,
                )
                for s in range(g, g + group)
            ],
            axis=0,
        )
        high, low = halves(values)
        h = jnp.dot(pick, high, preferred_element_type=f32)
        l = jnp.dot(pick, low, preferred_element_type=f32)
        total_h = h if total_h is None else total_h + h
        total_l = l if total_l is None else total_l + l
    dense = total_h + total_l
    out_ref[0, :, :] = dense[:, :order]
    out_ref[1, :, :] = dense[:, order:]


def place(arrived, slots, n_source, order, interpret=False):
    kernel = lambda *refs: place_kernel(slots, n_source, order, 4, *refs)
    return pl.pallas_call(
        kernel,
        out_shape=jax.ShapeDtypeStruct((2, 2 * order, order), f32),
        compiler_params=pltpu.CompilerParams(vmem_limit_bytes=32 << 20),
        interpret=interpret,
    )(arrived)


def screen_kernel(order, p_prev, p_here, p_next, v_prev, v_here, v_next, out_ref):
    b = order
    rows = lambda ref: ref[...].reshape(4 * b, b)
    flip = jnp.transpose
    vl_prev, vd, vl = v_prev[1], v_here[0], v_here[1]
    vd_next, vl_next = v_next[0], v_next[1]

    def upper(ref):
        return jnp.concatenate([-flip(ref[0, b:, :]), flip(ref[1, b:, :])], axis=0)

    vd_t, vl_h, vlp_t = halves(flip(vd)), halves(vl), halves(flip(vl_prev))
    from_prev = product(halves(rows(p_prev)), vlp_t)
    from_here = product(halves(rows(p_here)), vd_t)
    from_next = product(halves(rows(p_next)), vl_h)
    up_prev = product(halves(upper(p_prev)), vd_t)
    up_here = product(halves(upper(p_here)), vl_h)

    def beside(x, block):
        return jnp.concatenate(
            [x[block * b:(block + 1) * b], x[(2 + block) * b:(3 + block) * b]], axis=1
        )

    def pair(x):
        return jnp.concatenate([x[:b], x[b:]], axis=1)

    above = beside(from_prev, 0) + pair(up_prev)
    middle = beside(from_prev, 1) + beside(from_here, 0) + pair(up_here)
    below = beside(from_here, 1) + beside(from_next, 0)
    farther = beside(from_next, 1)
    stack = lambda *x: jnp.concatenate(x, axis=0)
    side = lambda *x: jnp.concatenate(x, axis=1)
    above, middle, below, farther = map(halves, (above, middle, below, farther))
    column = lambda *z: tuple(stack(*part) for part in zip(*z))
    diag = product(halves(side(vl_prev, vd, flip(vl))), column(above, middle, below))
    lower = product(halves(side(vl, vd_next, flip(vl_next))), column(middle, below, farther))
    for k, value in ((0, diag), (1, lower)):
        out_ref[k, 0, :, :] = value[:, :b]
        out_ref[k, 1, :, :] = value[:, b:]


def screen(p_prev, p_here, p_next, v_prev, v_here, v_next, interpret=False):
    b = v_here.shape[-1]
    kernel = lambda *refs: screen_kernel(b, *refs)
    return pl.pallas_call(
        kernel,
        out_shape=jax.ShapeDtypeStruct((2, 2, b, b), f32),
        compiler_params=pltpu.CompilerParams(vmem_limit_bytes=48 << 20),
        interpret=interpret,
    )(p_prev, p_here, p_next, v_prev, v_here, v_next)


def from_neighbours(value, axis):
    devices = lax.axis_size(axis)
    up = [(i, (i + 1) % devices) for i in range(devices)]
    down = [(j, i) for i, j in up]
    return lax.ppermute(value, axis, up), lax.ppermute(value, axis, down)


def body(g_lesser, g_greater, owner_tiles, energy_map, coulomb):
    slots, order = g_lesser.shape[1], g_lesser.shape[4]
    n_eb = lax.axis_size("eb")
    v_here = coulomb[0]
    v_prev, v_next = from_neighbours(v_here, "col")
    sent = correlate(g_lesser[0], g_greater[0], owner_tiles, energy_map, n_eb)
    sent, v_prev, v_next = lax.optimization_barrier((sent, v_prev, v_next))
    arrived = lax.all_to_all(
        sent.reshape(n_eb, 1, -1), "eb", split_axis=0, concat_axis=0, tiled=True
    )
    p_here = place(arrived.reshape(-1, LANES), slots, n_eb, order)
    p_prev, p_next = from_neighbours(p_here, "col")
    return screen(p_prev, p_here, p_next, v_prev, v_here, v_next)[None, None]


def solution(mesh):
    placed = (
        P("col", "eb", None, None, None),
        P("col", "eb", None, None, None),
        P("col", "eb"),
        P(),
        P("col", None, None, None),
    )
    return jax.shard_map(
        body,
        mesh=mesh,
        in_specs=placed,
        out_specs=P("eb", "col", None, None, None, None),
        check_vma=False,
    )
```

```python
import math

import jax
import jax.numpy as jnp
import numpy as np
from jax import lax
from jax.experimental import pallas as pl
from jax.experimental.pallas import tpu as pltpu
from jax.sharding import PartitionSpec as P

f32 = jnp.float32
bf16 = jnp.bfloat16
LANES = 128


def halves(x):
    high = x.astype(bf16)
    low = (x - high.astype(f32)).astype(bf16)
    return high, low


def product(a, b):
    (ah, al), (bh, bl) = a, b
    dot = lambda u, v: jnp.dot(u, v, preferred_element_type=f32)
    return dot(ah, bh) + (dot(ah, bl) + dot(al, bh))


def transform_tables(n_energy):
    k = np.arange(n_energy)
    angle = np.pi * (2 * k[:, None] + 1) * k[None, :] / (2 * n_energy)
    c, s = np.cos(angle), np.sin(angle)
    forward = np.concatenate([c, s], axis=0)
    scale = 2.0 / (2 * n_energy * math.sqrt(n_energy))
    backward = np.concatenate([c.T, -s.T], axis=1) * scale
    return forward.astype(np.float32), backward.astype(np.float32)


def numpy_halves(x):
    high = x.astype(bf16)
    low = (x - high.astype(np.float32)).astype(bf16)
    return high, low


def correlate_kernel(
    slots, unroll, n_energy, n_dest, stride,
    tiles_hbm, emap_hbm, forward_hbm, back_hbm, less_hbm, more_hbm,
    out_ref, tiles_ref, emap_ref, forward_ref, back_ref, less_ref, more_ref, back,
    small_sem, less_sem, more_sem,
):
    small = [
        pltpu.make_async_copy(source, target, small_sem.at[i])
        for i, (source, target) in enumerate(
            (
                (tiles_hbm, tiles_ref), (emap_hbm, emap_ref),
                (back_hbm, back_ref), (forward_hbm, forward_ref),
            )
        )
    ]

    def slot_copies(slot):
        return (
            pltpu.make_async_copy(less_hbm.at[slot], less_ref.at[slot], less_sem.at[slot]),
            pltpu.make_async_copy(more_hbm.at[slot], more_ref.at[slot], more_sem.at[slot]),
        )

    for copy in small:
        copy.start()
    for slot in range(slots):
        for copy in slot_copies(slot):
            copy.start()
    for copy in small:
        copy.wait()
    lane = lax.broadcasted_iota(jnp.int32, (1, LANES), 1)
    ids = jnp.zeros((1, LANES), jnp.int32)
    for slot in range(slots):
        ids = jnp.where(lane == slot, tiles_ref[0, slot], ids)
    out_ref[pl.ds(stride - 1, n_dest, stride=stride), :] = jnp.broadcast_to(
        ids.astype(f32), (n_dest, LANES)
    )
    row = jnp.broadcast_to(emap_ref[...], (n_dest, n_energy))
    i0 = lax.broadcasted_iota(jnp.int32, (n_dest, n_energy), 0)
    i1 = lax.broadcasted_iota(jnp.int32, (n_dest, n_energy), 1)
    column = jnp.sum(jnp.where(i0 == i1, row, 0), axis=1, keepdims=True)
    pick = jnp.where(i1 == column, 1.0, 0.0).astype(bf16)
    for part in range(2):
        back[part * n_dest:(part + 1) * n_dest, :] = jnp.dot(
            pick,
            back_ref[part * n_energy:(part + 1) * n_energy, :],
            preferred_element_type=f32,
        ).astype(bf16)

    def spectrum(ref, i):
        piece = lambda q: ref[i, pl.ds(q, n_energy, stride=4), :]
        high, low = halves(jnp.concatenate([piece(0), piece(2), piece(1), piece(3)], axis=1))
        value = jnp.dot(forward_ref[...], jnp.concatenate([high, high, low], axis=0), preferred_element_type=f32)
        half = value.shape[1] // 2
        return (
            value[:n_energy, :half], value[:n_energy, half:],
            value[n_energy:, :half], value[n_energy:, half:],
        )

    def one_slot(slot):
        for copy in slot_copies(slot):
            copy.wait()
        a, c, d, b = spectrum(less_ref, slot)
        e, g, h, f = spectrum(more_ref, slot)
        sum_re = a * e + b * f + c * g + d * h
        dif_re = a * f + b * e - c * h - d * g
        sum_im = c * e - d * f - a * g + b * h
        dif_im = c * f - d * e + a * h - b * g
        pairs = jnp.concatenate(
            [
                jnp.concatenate([sum_im, -dif_re], axis=0),
                jnp.concatenate([-sum_re, -dif_im], axis=0),
            ],
            axis=1,
        )
        high, low = halves(pairs)
        series = jnp.dot(
            back[...], jnp.concatenate([high, low], axis=0), preferred_element_type=f32
        )
        series = series[:n_dest] + series[n_dest:]
        for q in range(4):
            out_ref[pl.ds(slot * 4 + q, n_dest, stride=stride), :] = series[
                :, q * LANES:(q + 1) * LANES
            ]

    @pl.loop(0, slots // unroll)
    def _(step):
        for i in range(unroll):
            one_slot(step * unroll + i)


def correlate(less, more, tiles, emap, n_dest, interpret=False):
    slots, n_energy = less.shape[0], less.shape[1]
    stride = slots * 4 + 1
    unroll = 4
    forward, backward = transform_tables(n_energy)
    high, low = numpy_halves(forward)
    table = np.concatenate([high, low, high], axis=1)
    high, low = numpy_halves(backward)
    back = np.block([[high, high], [low, np.zeros_like(low)]])

    def packed(x):
        x = x.reshape(slots, n_energy, 2, 2, LANES).transpose(0, 1, 3, 2, 4)
        return x.reshape(slots, n_energy * 4, LANES)

    kernel = lambda *refs: correlate_kernel(
        slots, unroll, n_energy, n_dest, stride, *refs
    )
    hbm = pl.BlockSpec(memory_space=pltpu.HBM)
    rows = (slots, n_energy * 4, LANES)
    return pl.pallas_call(
        kernel,
        in_specs=[hbm] * 6,
        out_specs=pl.BlockSpec(memory_space=pltpu.VMEM),
        out_shape=jax.ShapeDtypeStruct((n_dest * stride, LANES), f32),
        scratch_shapes=[
            pltpu.SMEM((1, slots), jnp.int32),
            pltpu.VMEM((1, n_energy), jnp.int32),
            pltpu.VMEM(table.shape, bf16),
            pltpu.VMEM(back.shape, bf16),
            pltpu.VMEM(rows, f32),
            pltpu.VMEM(rows, f32),
            pltpu.VMEM((2 * n_dest, 4 * n_energy), bf16),
            pltpu.SemaphoreType.DMA((4,)),
            pltpu.SemaphoreType.DMA((slots,)),
            pltpu.SemaphoreType.DMA((slots,)),
        ],
        compiler_params=pltpu.CompilerParams(vmem_limit_bytes=32 << 20),
        interpret=interpret,
    )(*[
        pltpu.with_memory_space_constraint(x, pltpu.HBM)
        for x in (tiles, emap.reshape(1, n_energy), jnp.asarray(table), jnp.asarray(back),
                  packed(less), packed(more))
    ])


def place_kernel(slots, n_source, order, group, in_ref, diag_ref, lower_ref):
    stride = slots * 4 + 1
    ids = in_ref[pl.ds(stride - 1, n_source, stride=stride), :]
    by_slot = jnp.transpose(ids)
    total_h = total_l = None
    for g in range(0, slots, group):
        row = jnp.concatenate([by_slot[s:s + 1, :] for s in range(g, g + group)], axis=1)
        width = group * n_source
        tile = lax.broadcasted_iota(jnp.int32, (2 * order, width), 0).astype(f32)
        pick = jnp.where(tile == row, 1.0, 0.0).astype(bf16)
        values = jnp.concatenate(
            [
                jnp.concatenate(
                    [in_ref[pl.ds(s * 4 + q, n_source, stride=stride), :] for q in range(4)],
                    axis=1,
                )
                for s in range(g, g + group)
            ],
            axis=0,
        )
        high, low = halves(values)
        h = jnp.dot(pick, high, preferred_element_type=f32)
        l = jnp.dot(pick, low, preferred_element_type=f32)
        total_h = h if total_h is None else total_h + h
        total_l = l if total_l is None else total_l + l
    dense = total_h + total_l
    for k, out_ref in ((0, diag_ref), (1, lower_ref)):
        for part in range(2):
            out_ref[part, :, :] = dense[
                k * order:(k + 1) * order, part * order:(part + 1) * order
            ]


def place(arrived, slots, n_source, order, interpret=False):
    kernel = lambda *refs: place_kernel(slots, n_source, order, 4, *refs)
    return pl.pallas_call(
        kernel,
        out_shape=[jax.ShapeDtypeStruct((2, order, order), f32)] * 2,
        compiler_params=pltpu.CompilerParams(vmem_limit_bytes=32 << 20),
        interpret=interpret,
    )(arrived)


def joined(x, axis):
    return jnp.concatenate([x[0], x[1]], axis=axis)


def right(parts, weight):
    rows = jnp.concatenate([joined(x, 0) for x in parts], axis=0)
    value = product(halves(rows), weight)
    n = parts[0].shape[1]
    pieces = [value[i * n:(i + 1) * n] for i in range(2 * len(parts))]
    return [
        jnp.concatenate(pieces[2 * i:2 * i + 2], axis=1) for i in range(len(parts))
    ]


def left(weights, value):
    high, low = halves(jnp.concatenate(weights, axis=0))
    vh, vl = halves(value)
    rows = high.shape[0]
    dot = lambda u, v: jnp.dot(u, v, preferred_element_type=f32)
    first = dot(jnp.concatenate([high, low], axis=0), vh)
    total = first[:rows] + (first[rows:] + dot(high, vl))
    n = weights[0].shape[0]
    return [total[i * n:(i + 1) * n] for i in range(len(weights))]


def upper(lower):
    return jnp.stack([-jnp.transpose(lower[0]), jnp.transpose(lower[1])])


def store(ref, value):
    n = ref.shape[-1]
    ref[0, :, :] = value[:, :n]
    ref[1, :, :] = value[:, n:]


def local_kernel(diag_ref, lower_ref, v_prev, v_here, up_ref, down_ref, middle_ref, below_ref):
    diag, lower = diag_ref[...], lower_ref[...]
    vd, vl = v_here[0], v_here[1]
    vl_half = halves(vl)
    (for_up,) = right([diag], halves(jnp.transpose(vl)))
    (for_up,) = left([vl], for_up)
    store(up_ref, for_up)
    (for_down,) = right([diag], halves(v_prev[1]))
    store(down_ref, for_down)
    middle, below = right([diag, lower], halves(jnp.transpose(vd)))
    (from_upper,) = right([upper(lower)], vl_half)
    middle_ref[...] = middle + from_upper
    below_ref[...] = below


def lower_kernel(prev_ref, next_ref, middle_ref, v_prev, v_here, v_next, diag_ref, lower_ref):
    prev = prev_ref[...]
    vl_prev, vd, vl, vl_next = v_prev[1], v_here[0], v_here[1], v_next[1]
    (above,) = right([upper(prev)], halves(jnp.transpose(vd)))
    (middle,) = right([prev], halves(jnp.transpose(vl_prev)))
    (farther,) = right([next_ref[...]], halves(vl))
    diag, lower = left([vd, vl], middle + middle_ref[...])
    diag_ref[...] = diag + left([vl_prev], above)[0]
    lower_ref[...] = lower + left([jnp.transpose(vl_next)], farther)[0]


def last_kernel(prev_ref, next_ref, below_ref, diag_ref, lower_ref, v_here, v_next, out_ref):
    below = below_ref[...] + joined(next_ref[...], 1)
    diag, lower = left([jnp.transpose(v_here[1]), v_next[0]], below)
    store(out_ref.at[0], diag + (diag_ref[...] + joined(prev_ref[...], 1)))
    store(out_ref.at[1], lower + lower_ref[...])


def block_call(kernel, outs, products, interpret, *args):
    shapes = [jax.ShapeDtypeStruct(shape, f32) for shape in outs]
    order = outs[0][-2]
    return pl.pallas_call(
        kernel,
        out_shape=shapes,
        compiler_params=pltpu.CompilerParams(vmem_limit_bytes=32 << 20),
        cost_estimate=pl.CostEstimate(
            flops=products * 3 * 4 * order**3,
            bytes_accessed=sum(4 * math.prod(x.shape) for x in (*args, *shapes)),
            transcendentals=0,
        ),
        interpret=interpret,
    )(*args)


def shifted(value, axis, step):
    devices = lax.axis_size(axis)
    return lax.ppermute(value, axis, [(i, (i + step) % devices) for i in range(devices)])


def screen(diag, lower, v_prev, v_here, v_next, shift, interpret=False):
    b = v_here.shape[-1]
    block, wide = (2, b, b), (b, 2 * b)
    lower_prev, lower_next = shift(lower, 1), shift(lower, -1)
    for_up, for_down, middle, below = block_call(
        local_kernel, (block, block, wide, wide), 6, interpret, diag, lower, v_prev, v_here
    )
    diag_prev, diag_next = shift(for_up, 1), shift(for_down, -1)
    diag_part, lower_part = block_call(
        lower_kernel, (wide, wide), 7, interpret,
        lower_prev, lower_next, middle, v_prev, v_here, v_next,
    )
    (result,) = block_call(
        last_kernel, ((2, 2, b, b),), 2, interpret,
        diag_prev, diag_next, below, diag_part, lower_part, v_here, v_next,
    )
    return result


def body(g_lesser, g_greater, owner_tiles, energy_map, coulomb):
    slots, order = g_lesser.shape[1], g_lesser.shape[4]
    n_eb = lax.axis_size("eb")
    shift = lambda value, step: shifted(value, "col", step)
    v_here = coulomb[0]
    v_prev, v_next = shift(v_here, 1), shift(v_here, -1)
    sent = correlate(g_lesser[0], g_greater[0], owner_tiles, energy_map, n_eb)
    sent, v_prev, v_next = lax.optimization_barrier((sent, v_prev, v_next))
    arrived = lax.all_to_all(
        sent.reshape(n_eb, 1, -1), "eb", split_axis=0, concat_axis=0, tiled=True
    )
    diag, lower = place(arrived.reshape(-1, LANES), slots, n_eb, order)
    return screen(diag, lower, v_prev, v_here, v_next, shift)[None, None]


def solution(mesh):
    placed = (
        P("col", "eb", None, None, None),
        P("col", "eb", None, None, None),
        P("col", "eb"),
        P(),
        P("col", None, None, None),
    )
    return jax.shard_map(
        body,
        mesh=mesh,
        in_specs=placed,
        out_specs=P("eb", "col", None, None, None, None),
        check_vma=False,
    )
```

```python
import functools
import math

import jax
import jax.numpy as jnp
import numpy as np
from jax import lax
from jax.experimental import pallas as pl
from jax.experimental.pallas import tpu as pltpu
from jax.sharding import PartitionSpec as P

f32 = jnp.float32
bf16 = jnp.bfloat16
LANES = 128


def halves(x):
    high = x.astype(bf16)
    low = (x - high.astype(f32)).astype(bf16)
    return high, low


def product(a, b):
    (ah, al), (bh, bl) = a, b
    dot = lambda u, v: jnp.dot(u, v, preferred_element_type=f32)
    return dot(ah, bh) + (dot(ah, bl) + dot(al, bh))


def transform_tables(n_energy):
    k = np.arange(n_energy)
    angle = np.pi * (2 * k[:, None] + 1) * k[None, :] / (2 * n_energy)
    c, s = np.cos(angle), np.sin(angle)
    forward = np.concatenate([c, s], axis=0)
    scale = 2.0 / (2 * n_energy * math.sqrt(n_energy))
    backward = np.concatenate([c.T, -s.T], axis=1) * scale
    return forward.astype(np.float32), backward.astype(np.float32)


def numpy_halves(x):
    high = x.astype(bf16)
    low = (x - high.astype(np.float32)).astype(bf16)
    return high, low


def correlate_kernel(
    slots, unroll, n_energy, n_dest, stride,
    tiles_hbm, emap_hbm, forward_hbm, back_hbm, less_hbm, more_hbm,
    out_ref, tiles_ref, emap_ref, forward_ref, back_ref, less_ref, more_ref, back,
    small_sem, less_sem, more_sem,
):
    small = [
        pltpu.make_async_copy(source, target, small_sem.at[i])
        for i, (source, target) in enumerate(
            (
                (tiles_hbm, tiles_ref), (emap_hbm, emap_ref),
                (back_hbm, back_ref), (forward_hbm, forward_ref),
            )
        )
    ]

    def slot_copies(slot):
        return (
            pltpu.make_async_copy(less_hbm.at[slot], less_ref.at[slot], less_sem.at[slot]),
            pltpu.make_async_copy(more_hbm.at[slot], more_ref.at[slot], more_sem.at[slot]),
        )

    for copy in small:
        copy.start()
    for slot in range(slots):
        for copy in slot_copies(slot):
            copy.start()
    for copy in small:
        copy.wait()
    lane = lax.broadcasted_iota(jnp.int32, (1, LANES), 1)
    ids = jnp.zeros((1, LANES), jnp.int32)
    for slot in range(slots):
        ids = jnp.where(lane == slot, tiles_ref[0, slot], ids)
    out_ref[pl.ds(stride - 1, n_dest, stride=stride), :] = jnp.broadcast_to(
        ids.astype(f32), (n_dest, LANES)
    )
    row = jnp.broadcast_to(emap_ref[...], (n_dest, n_energy))
    i0 = lax.broadcasted_iota(jnp.int32, (n_dest, n_energy), 0)
    i1 = lax.broadcasted_iota(jnp.int32, (n_dest, n_energy), 1)
    column = jnp.sum(jnp.where(i0 == i1, row, 0), axis=1, keepdims=True)
    pick = jnp.where(i1 == column, 1.0, 0.0).astype(bf16)
    for part in range(2):
        back[part * n_dest:(part + 1) * n_dest, :] = jnp.dot(
            pick,
            back_ref[part * n_energy:(part + 1) * n_energy, :],
            preferred_element_type=f32,
        ).astype(bf16)

    def pieces(ref, first):
        read = lambda slot, q: ref[slot, pl.ds(q, n_energy, stride=4), :]
        return jnp.concatenate(
            [read(first + i, q) for qs in ((0, 2), (1, 3)) for i in range(unroll) for q in qs],
            axis=1,
        )

    def spectrum(ref, first):
        high, low = halves(pieces(ref, first))
        value = jnp.dot(
            forward_ref[...],
            jnp.concatenate([high, high, low], axis=0),
            preferred_element_type=f32,
        )
        half = value.shape[1] // 2
        return (
            value[:n_energy, :half], value[:n_energy, half:],
            value[n_energy:, :half], value[n_energy:, half:],
        )

    def batch(first):
        a, c, d, b = spectrum(less_ref, first)
        e, g, h, f = spectrum(more_ref, first)
        sum_re = a * e + b * f + c * g + d * h
        dif_re = a * f + b * e - c * h - d * g
        sum_im = c * e - d * f - a * g + b * h
        dif_im = c * f - d * e + a * h - b * g
        pairs = jnp.concatenate(
            [
                jnp.concatenate([sum_im, -dif_re], axis=0),
                jnp.concatenate([-sum_re, -dif_im], axis=0),
            ],
            axis=1,
        )
        high, low = halves(pairs)
        series = jnp.dot(
            back[...], jnp.concatenate([high, low], axis=0), preferred_element_type=f32
        )
        series = series[:n_dest] + series[n_dest:]
        for i in range(unroll):
            for q in range(4):
                at = ((q // 2) * 2 * unroll + 2 * i + q % 2) * LANES
                out_ref[pl.ds((first + i) * 4 + q, n_dest, stride=stride), :] = series[
                    :, at:at + LANES
                ]

    @pl.loop(0, slots // unroll)
    def _(step):
        for i in range(unroll):
            for copy in slot_copies(step * unroll + i):
                copy.wait()
        batch(step * unroll)


def correlate(less, more, tiles, emap, n_dest, interpret=False):
    slots, n_energy = less.shape[0], less.shape[1]
    stride = slots * 4 + 1
    unroll = 6
    forward, backward = transform_tables(n_energy)
    high, low = numpy_halves(forward)
    table = np.concatenate([high, low, high], axis=1)
    high, low = numpy_halves(backward)
    back = np.block([[high, high], [low, np.zeros_like(low)]])

    def packed(x):
        x = x.reshape(slots, n_energy, 2, 2, LANES).transpose(0, 1, 3, 2, 4)
        return x.reshape(slots, n_energy * 4, LANES)

    kernel = lambda *refs: correlate_kernel(
        slots, unroll, n_energy, n_dest, stride, *refs
    )
    hbm = pl.BlockSpec(memory_space=pltpu.HBM)
    rows = (slots, n_energy * 4, LANES)
    return pl.pallas_call(
        kernel,
        in_specs=[hbm] * 6,
        out_specs=pl.BlockSpec(memory_space=pltpu.VMEM),
        out_shape=jax.ShapeDtypeStruct((n_dest * stride, LANES), f32),
        scratch_shapes=[
            pltpu.SMEM((1, slots), jnp.int32),
            pltpu.VMEM((1, n_energy), jnp.int32),
            pltpu.VMEM(table.shape, bf16),
            pltpu.VMEM(back.shape, bf16),
            pltpu.VMEM(rows, f32),
            pltpu.VMEM(rows, f32),
            pltpu.VMEM((2 * n_dest, 4 * n_energy), bf16),
            pltpu.SemaphoreType.DMA((4,)),
            pltpu.SemaphoreType.DMA((slots,)),
            pltpu.SemaphoreType.DMA((slots,)),
        ],
        compiler_params=pltpu.CompilerParams(vmem_limit_bytes=32 << 20),
        interpret=interpret,
    )(*[
        pltpu.with_memory_space_constraint(x, pltpu.HBM)
        for x in (tiles, emap.reshape(1, n_energy), jnp.asarray(table), jnp.asarray(back),
                  packed(less), packed(more))
    ])


def placed(block, slots, n_source, order, group, in_ref):
    stride = slots * 4 + 1
    ids = in_ref[pl.ds(stride - 1, n_source, stride=stride), :]
    by_slot = jnp.transpose(ids)
    total = None
    for g in range(0, slots, group):
        row = jnp.concatenate([by_slot[s:s + 1, :] for s in range(g, g + group)], axis=1)
        tile = lax.broadcasted_iota(jnp.int32, (order, group * n_source), 0) + block * order
        pick = jnp.where(tile.astype(f32) == row, 1.0, 0.0).astype(bf16)
        values = jnp.concatenate(
            [
                jnp.concatenate(
                    [in_ref[pl.ds(s * 4 + q, n_source, stride=stride), :] for q in range(4)],
                    axis=1,
                )
                for s in range(g, g + group)
            ],
            axis=0,
        )
        parts = [jnp.dot(pick, x, preferred_element_type=f32) for x in halves(values)]
        total = parts if total is None else [t + x for t, x in zip(total, parts)]
    return total[0] + total[1]


def joined(x, axis):
    return jnp.concatenate([x[0], x[1]], axis=axis)


def right(parts, weight):
    rows = jnp.concatenate([joined(x, 0) for x in parts], axis=0)
    value = product(halves(rows), weight)
    n = parts[0].shape[1]
    pieces = [value[i * n:(i + 1) * n] for i in range(2 * len(parts))]
    return [
        jnp.concatenate(pieces[2 * i:2 * i + 2], axis=1) for i in range(len(parts))
    ]


def left(weights, value):
    high, low = halves(jnp.concatenate(weights, axis=0))
    vh, vl = halves(value)
    rows = high.shape[0]
    dot = lambda u, v: jnp.dot(u, v, preferred_element_type=f32)
    first = dot(jnp.concatenate([high, low], axis=0), vh)
    total = first[:rows] + (first[rows:] + dot(high, vl))
    n = weights[0].shape[0]
    return [total[i * n:(i + 1) * n] for i in range(len(weights))]


def upper(lower):
    return jnp.stack([-jnp.transpose(lower[0]), jnp.transpose(lower[1])])


def store(ref, value):
    n = ref.shape[-1]
    ref[0, :, :] = value[:, :n]
    ref[1, :, :] = value[:, n:]


def first_kernel(rows, in_ref, lower_ref):
    store(lower_ref, placed(1, *rows, in_ref))


def local_kernel(
    rows, in_ref, lower_ref, v_prev, v_here, up_ref, down_ref, middle_ref, below_ref
):
    order = lower_ref.shape[-1]
    diag = placed(0, *rows, in_ref)
    diag = jnp.stack([diag[:, :order], diag[:, order:]])
    lower = lower_ref[...]
    vd, vl = v_here[0], v_here[1]
    vl_half = halves(vl)
    (for_up,) = right([diag], halves(jnp.transpose(vl)))
    (for_up,) = left([vl], for_up)
    store(up_ref, for_up)
    (for_down,) = right([diag], halves(v_prev[1]))
    store(down_ref, for_down)
    middle, below = right([diag, lower], halves(jnp.transpose(vd)))
    (from_upper,) = right([upper(lower)], vl_half)
    middle_ref[...] = middle + from_upper
    below_ref[...] = below


def lower_kernel(prev_ref, next_ref, middle_ref, v_prev, v_here, v_next, diag_ref, lower_ref):
    prev = prev_ref[...]
    vl_prev, vd, vl, vl_next = v_prev[1], v_here[0], v_here[1], v_next[1]
    (above,) = right([upper(prev)], halves(jnp.transpose(vd)))
    (middle,) = right([prev], halves(jnp.transpose(vl_prev)))
    (farther,) = right([next_ref[...]], halves(vl))
    diag, lower = left([vd, vl], middle + middle_ref[...])
    diag_ref[...] = diag + left([vl_prev], above)[0]
    lower_ref[...] = lower + left([jnp.transpose(vl_next)], farther)[0]


def last_kernel(prev_ref, next_ref, below_ref, diag_ref, lower_ref, v_here, v_next, out_ref):
    below = below_ref[...] + joined(next_ref[...], 1)
    diag, lower = left([jnp.transpose(v_here[1]), v_next[0]], below)
    store(out_ref.at[0], diag + (diag_ref[...] + joined(prev_ref[...], 1)))
    store(out_ref.at[1], lower + lower_ref[...])


def block_call(kernel, outs, products, interpret, *args):
    shapes = [jax.ShapeDtypeStruct(shape, f32) for shape in outs]
    order = outs[0][-2]
    return pl.pallas_call(
        kernel,
        out_shape=shapes,
        compiler_params=pltpu.CompilerParams(vmem_limit_bytes=32 << 20),
        cost_estimate=pl.CostEstimate(
            flops=products * 3 * 4 * order**3,
            bytes_accessed=sum(4 * math.prod(x.shape) for x in (*args, *shapes)),
            transcendentals=0,
        ),
        interpret=interpret,
    )(*args)


def shifted(value, axis, step):
    devices = lax.axis_size(axis)
    return lax.ppermute(value, axis, [(i, (i + step) % devices) for i in range(devices)])


def screen(arrived, slots, n_source, v_prev, v_here, v_next, shift, interpret=False):
    b = v_here.shape[-1]
    block, wide = (2, b, b), (b, 2 * b)
    rows = (slots, n_source, b, 4)
    (lower,) = block_call(
        functools.partial(first_kernel, rows), (block,), 2, interpret, arrived
    )
    lower_prev, lower_next = shift(lower, 1), shift(lower, -1)
    for_up, for_down, middle, below = block_call(
        functools.partial(local_kernel, rows), (block, block, wide, wide), 8, interpret,
        arrived, lower, v_prev, v_here,
    )
    diag_prev, diag_next = shift(for_up, 1), shift(for_down, -1)
    diag_part, lower_part = block_call(
        lower_kernel, (wide, wide), 7, interpret,
        lower_prev, lower_next, middle, v_prev, v_here, v_next,
    )
    (result,) = block_call(
        last_kernel, ((2, 2, b, b),), 2, interpret,
        diag_prev, diag_next, below, diag_part, lower_part, v_here, v_next,
    )
    return result


def body(g_lesser, g_greater, owner_tiles, energy_map, coulomb):
    slots = g_lesser.shape[1]
    n_eb = lax.axis_size("eb")
    shift = lambda value, step: shifted(value, "col", step)
    v_here = coulomb[0]
    sent = correlate(g_lesser[0], g_greater[0], owner_tiles, energy_map, n_eb)
    sent, v_moved = lax.optimization_barrier((sent, v_here))
    v_prev, v_next = shift(v_moved, 1), shift(v_moved, -1)
    arrived = lax.all_to_all(
        sent.reshape(n_eb, 1, -1), "eb", split_axis=0, concat_axis=0, tiled=True
    )
    arrived, v_prev, v_next = lax.optimization_barrier((arrived, v_prev, v_next))
    arrived = arrived.reshape(-1, LANES)
    return screen(arrived, slots, n_eb, v_prev, v_here, v_next, shift)[None, None]


def solution(mesh):
    placed = (
        P("col", "eb", None, None, None),
        P("col", "eb", None, None, None),
        P("col", "eb"),
        P(),
        P("col", None, None, None),
    )
    return jax.shard_map(
        body,
        mesh=mesh,
        in_specs=placed,
        out_specs=P("eb", "col", None, None, None, None),
        check_vma=False,
    )
```

```python
import functools
import math

import jax
import jax.numpy as jnp
import numpy as np
from jax import lax
from jax.experimental import pallas as pl
from jax.experimental.pallas import tpu as pltpu
from jax.sharding import PartitionSpec as P

f32 = jnp.float32
bf16 = jnp.bfloat16
LANES = 128


def halves(x):
    high = x.astype(bf16)
    low = (x - high.astype(f32)).astype(bf16)
    return high, low


def product(a, b):
    (ah, al), (bh, bl) = a, b
    dot = lambda u, v: jnp.dot(u, v, preferred_element_type=f32)
    return dot(ah, bh) + (dot(ah, bl) + dot(al, bh))


def transform_tables(n_energy):
    k = np.arange(n_energy)
    angle = np.pi * (2 * k[:, None] + 1) * k[None, :] / (2 * n_energy)
    c, s = np.cos(angle), np.sin(angle)
    forward = np.concatenate([c, s], axis=0)
    scale = 2.0 / (2 * n_energy * math.sqrt(n_energy))
    backward = np.concatenate([c.T, -s.T], axis=1) * scale
    return forward.astype(np.float32), backward.astype(np.float32)


def numpy_halves(x):
    high = x.astype(bf16)
    low = (x - high.astype(np.float32)).astype(bf16)
    return high, low


def correlate_kernel(
    slots, sizes, n_energy, n_dest, stride,
    tiles_hbm, emap_hbm, forward_hbm, back_hbm, less_hbm, more_hbm,
    out_ref, tiles_ref, emap_ref, forward_ref, back_ref, less_ref, more_ref, back,
    small_sem, less_sem, more_sem,
):
    small = [
        pltpu.make_async_copy(source, target, small_sem.at[i])
        for i, (source, target) in enumerate(
            (
                (tiles_hbm, tiles_ref), (emap_hbm, emap_ref),
                (back_hbm, back_ref), (forward_hbm, forward_ref),
            )
        )
    ]

    def slot_copies(slot):
        return (
            pltpu.make_async_copy(less_hbm.at[slot], less_ref.at[slot], less_sem.at[slot]),
            pltpu.make_async_copy(more_hbm.at[slot], more_ref.at[slot], more_sem.at[slot]),
        )

    for copy in small:
        copy.start()
    for slot in range(slots):
        for copy in slot_copies(slot):
            copy.start()
    for copy in small:
        copy.wait()
    lane = lax.broadcasted_iota(jnp.int32, (1, LANES), 1)
    ids = jnp.zeros((1, LANES), jnp.int32)
    for slot in range(slots):
        ids = jnp.where(lane == slot, tiles_ref[0, slot], ids)
    out_ref[pl.ds(stride - 1, n_dest, stride=stride), :] = jnp.broadcast_to(
        ids.astype(f32), (n_dest, LANES)
    )
    row = jnp.broadcast_to(emap_ref[...], (n_dest, n_energy))
    i0 = lax.broadcasted_iota(jnp.int32, (n_dest, n_energy), 0)
    i1 = lax.broadcasted_iota(jnp.int32, (n_dest, n_energy), 1)
    column = jnp.sum(jnp.where(i0 == i1, row, 0), axis=1, keepdims=True)
    pick = jnp.where(i1 == column, 1.0, 0.0).astype(bf16)
    for part in range(2):
        back[part * n_dest:(part + 1) * n_dest, :] = jnp.dot(
            pick,
            back_ref[part * n_energy:(part + 1) * n_energy, :],
            preferred_element_type=f32,
        ).astype(bf16)

    def pieces(ref, first, size):
        read = lambda slot, q: ref[slot, pl.ds(q, n_energy, stride=4), :]
        return jnp.concatenate(
            [read(first + i, q) for qs in ((0, 2), (1, 3)) for i in range(size) for q in qs],
            axis=1,
        )

    def spectrum(ref, first, size):
        high, low = halves(pieces(ref, first, size))
        value = jnp.dot(
            forward_ref[...],
            jnp.concatenate([high, high, low], axis=0),
            preferred_element_type=f32,
        )
        half = value.shape[1] // 2
        return (
            value[:n_energy, :half], value[:n_energy, half:],
            value[n_energy:, :half], value[n_energy:, half:],
        )

    def batch(first, size):
        a, c, d, b = spectrum(less_ref, first, size)
        e, g, h, f = spectrum(more_ref, first, size)
        sum_re = a * e + b * f + c * g + d * h
        dif_re = a * f + b * e - c * h - d * g
        sum_im = c * e - d * f - a * g + b * h
        dif_im = c * f - d * e + a * h - b * g
        pairs = jnp.concatenate(
            [
                jnp.concatenate([sum_im, -dif_re], axis=0),
                jnp.concatenate([-sum_re, -dif_im], axis=0),
            ],
            axis=1,
        )
        high, low = halves(pairs)
        series = jnp.dot(
            back[...], jnp.concatenate([high, low], axis=0), preferred_element_type=f32
        )
        series = series[:n_dest] + series[n_dest:]
        for i in range(size):
            for q in range(4):
                at = ((q // 2) * 2 * size + 2 * i + q % 2) * LANES
                out_ref[pl.ds((first + i) * 4 + q, n_dest, stride=stride), :] = series[
                    :, at:at + LANES
                ]

    first = 0
    for size in sizes:
        for slot in range(first, first + size):
            for copy in slot_copies(slot):
                copy.wait()
        batch(first, size)
        first += size


def correlate(less, more, tiles, emap, n_dest, interpret=False):
    slots, n_energy = less.shape[0], less.shape[1]
    stride = slots * 4 + 1
    sizes = (4, 8)
    forward, backward = transform_tables(n_energy)
    high, low = numpy_halves(forward)
    table = np.concatenate([high, low, high], axis=1)
    high, low = numpy_halves(backward)
    back = np.block([[high, high], [low, np.zeros_like(low)]])

    def packed(x):
        x = x.reshape(slots, n_energy, 2, 2, LANES).transpose(0, 1, 3, 2, 4)
        return x.reshape(slots, n_energy * 4, LANES)

    kernel = lambda *refs: correlate_kernel(
        slots, sizes, n_energy, n_dest, stride, *refs
    )
    hbm = pl.BlockSpec(memory_space=pltpu.HBM)
    rows = (slots, n_energy * 4, LANES)
    return pl.pallas_call(
        kernel,
        in_specs=[hbm] * 6,
        out_specs=pl.BlockSpec(memory_space=pltpu.VMEM),
        out_shape=pltpu.VMEM((n_dest * stride, LANES), f32),
        scratch_shapes=[
            pltpu.SMEM((1, slots), jnp.int32),
            pltpu.VMEM((1, n_energy), jnp.int32),
            pltpu.VMEM(table.shape, bf16),
            pltpu.VMEM(back.shape, bf16),
            pltpu.VMEM(rows, f32),
            pltpu.VMEM(rows, f32),
            pltpu.VMEM((2 * n_dest, 4 * n_energy), bf16),
            pltpu.SemaphoreType.DMA((4,)),
            pltpu.SemaphoreType.DMA((slots,)),
            pltpu.SemaphoreType.DMA((slots,)),
        ],
        compiler_params=pltpu.CompilerParams(vmem_limit_bytes=32 << 20),
        interpret=interpret,
    )(*[
        pltpu.with_memory_space_constraint(x, pltpu.HBM)
        for x in (tiles, emap.reshape(1, n_energy), jnp.asarray(table), jnp.asarray(back),
                  packed(less), packed(more))
    ])


def placed(block, slots, n_source, order, group, in_ref):
    stride = slots * 4 + 1
    ids = in_ref[pl.ds(stride - 1, n_source, stride=stride), :]
    by_slot = jnp.transpose(ids)
    total = None
    for g in range(0, slots, group):
        row = jnp.concatenate([by_slot[s:s + 1, :] for s in range(g, g + group)], axis=1)
        tile = lax.broadcasted_iota(jnp.int32, (order, group * n_source), 0) + block * order
        pick = jnp.where(tile.astype(f32) == row, 1.0, 0.0).astype(bf16)
        values = jnp.concatenate(
            [
                jnp.concatenate(
                    [in_ref[pl.ds(s * 4 + q, n_source, stride=stride), :] for q in range(4)],
                    axis=1,
                )
                for s in range(g, g + group)
            ],
            axis=0,
        )
        parts = [jnp.dot(pick, x, preferred_element_type=f32) for x in halves(values)]
        total = parts if total is None else [t + x for t, x in zip(total, parts)]
    return total[0] + total[1]


def joined(x, axis):
    return jnp.concatenate([x[0], x[1]], axis=axis)


def right(parts, weight):
    rows = jnp.concatenate([joined(x, 0) for x in parts], axis=0)
    value = product(halves(rows), weight)
    n = parts[0].shape[1]
    pieces = [value[i * n:(i + 1) * n] for i in range(2 * len(parts))]
    return [
        jnp.concatenate(pieces[2 * i:2 * i + 2], axis=1) for i in range(len(parts))
    ]


def stacked(weights):
    return jnp.concatenate(halves(jnp.concatenate(weights, axis=0)), axis=0)


def times(weights, high, low):
    rows = weights.shape[0] // 2
    dot = lambda u, v: jnp.dot(u, v, preferred_element_type=f32)
    first = dot(weights, high)
    return first[:rows] + (first[rows:] + dot(weights[:rows], low))


def left(weights, value):
    total = times(stacked(weights), *halves(value))
    n = weights[0].shape[0]
    return [total[i * n:(i + 1) * n] for i in range(len(weights))]


def upper(lower):
    return jnp.stack([-jnp.transpose(lower[0]), jnp.transpose(lower[1])])


def store(ref, value):
    n = ref.shape[-1]
    ref[0, :, :] = value[:, :n]
    ref[1, :, :] = value[:, n:]


def first_kernel(rows, in_ref, lower_ref):
    store(lower_ref, placed(1, *rows, in_ref))


def local_kernel(
    rows, in_ref, lower_ref, v_prev, v_here, up_ref, down_ref, middle_ref, below_ref
):
    order = lower_ref.shape[-1]
    diag = placed(0, *rows, in_ref)
    diag = jnp.stack([diag[:, :order], diag[:, order:]])
    lower = lower_ref[...]
    vd, vl = v_here[0], v_here[1]
    vl_half = halves(vl)
    (for_up,) = right([diag], halves(jnp.transpose(vl)))
    (for_up,) = left([vl], for_up)
    store(up_ref, for_up)
    (for_down,) = right([diag], halves(v_prev[1]))
    store(down_ref, for_down)
    middle, below = right([diag, lower], halves(jnp.transpose(vd)))
    (from_upper,) = right([upper(lower)], vl_half)
    middle_ref[...] = middle + from_upper
    below_ref[...] = below


def lower_kernel(
    prev_ref, next_ref, middle_ref, v_prev, v_here, v_next,
    diag_ref, lower_ref, diag_w, lower_w,
):
    diag_w[...] = stacked([jnp.transpose(v_here[1])])
    lower_w[...] = stacked([v_next[0]])
    prev = prev_ref[...]
    vl_prev, vd, vl, vl_next = v_prev[1], v_here[0], v_here[1], v_next[1]
    (above,) = right([upper(prev)], halves(jnp.transpose(vd)))
    (middle,) = right([prev], halves(jnp.transpose(vl_prev)))
    (farther,) = right([next_ref[...]], halves(vl))
    diag, lower = left([vd, vl], middle + middle_ref[...])
    diag_ref[...] = diag + left([vl_prev], above)[0]
    lower_ref[...] = lower + left([jnp.transpose(vl_next)], farther)[0]


def last_kernel(
    prev_ref, next_ref, below_ref, diag_ref, lower_ref, diag_w, lower_w,
    out_hbm, buffer, sems,
):
    high, low = halves(below_ref[...] + joined(next_ref[...], 1))
    copies = [pltpu.make_async_copy(buffer.at[k], out_hbm.at[k], sems.at[k]) for k in range(2)]
    diag = times(diag_w[...], high, low)
    store(buffer.at[0], diag + (diag_ref[...] + joined(prev_ref[...], 1)))
    copies[0].start()
    store(buffer.at[1], times(lower_w[...], high, low) + lower_ref[...])
    copies[1].start()
    for copy in copies:
        copy.wait()


def block_call(kernel, outs, products, interpret, *args, **options):
    shapes = [
        out if isinstance(out, jax.ShapeDtypeStruct) else jax.ShapeDtypeStruct(out, f32)
        for out in outs
    ]
    order = args[-1].shape[-1]
    return pl.pallas_call(
        kernel,
        out_shape=shapes,
        **options,
        compiler_params=pltpu.CompilerParams(vmem_limit_bytes=32 << 20),
        cost_estimate=pl.CostEstimate(
            flops=products * 3 * 4 * order**3,
            bytes_accessed=sum(4 * math.prod(x.shape) for x in (*args, *shapes)),
            transcendentals=0,
        ),
        interpret=interpret,
    )(*args)


def shifted(value, axis, step):
    devices = lax.axis_size(axis)
    return lax.ppermute(value, axis, [(i, (i + step) % devices) for i in range(devices)])


def screen(arrived, slots, n_source, v_prev, v_here, v_next, shift, interpret=False):
    b = v_here.shape[-1]
    block, wide = (2, b, b), (b, 2 * b)
    rows = (slots, n_source, b, 4)
    (lower,) = block_call(
        functools.partial(first_kernel, rows), (block,), 2, interpret, arrived
    )
    lower_prev, lower_next = shift(lower, 1), shift(lower, -1)
    for_up, for_down, middle, below = block_call(
        functools.partial(local_kernel, rows), (block, block, wide, wide), 8, interpret,
        arrived, lower, v_prev, v_here,
    )
    diag_prev, diag_next = shift(for_up, 1), shift(for_down, -1)
    weights = jax.ShapeDtypeStruct((2 * b, b), bf16)
    diag_part, lower_part, diag_w, lower_w = block_call(
        lower_kernel, (wide, wide, weights, weights), 7, interpret,
        lower_prev, lower_next, middle, v_prev, v_here, v_next,
    )
    (result,) = block_call(
        last_kernel, ((2, 2, b, b),), 2, interpret,
        diag_prev, diag_next, below, diag_part, lower_part, diag_w, lower_w,
        out_specs=[pl.BlockSpec(memory_space=pltpu.HBM)],
        scratch_shapes=[pltpu.VMEM((2, 2, b, b), f32), pltpu.SemaphoreType.DMA((2,))],
    )
    return result


def body(g_lesser, g_greater, owner_tiles, energy_map, coulomb):
    slots = g_lesser.shape[1]
    n_eb = lax.axis_size("eb")
    shift = lambda value, step: shifted(value, "col", step)
    v_here = coulomb[0]
    sent = correlate(g_lesser[0], g_greater[0], owner_tiles, energy_map, n_eb)
    sent, v_moved = lax.optimization_barrier((sent, v_here))
    v_prev, v_next = shift(v_moved, 1), shift(v_moved, -1)
    arrived = lax.all_to_all(
        sent.reshape(n_eb, 1, -1), "eb", split_axis=0, concat_axis=0, tiled=True
    )
    arrived, v_prev, v_next = lax.optimization_barrier((arrived, v_prev, v_next))
    arrived = arrived.reshape(-1, LANES)
    return screen(arrived, slots, n_eb, v_prev, v_here, v_next, shift)[None, None]


def solution(mesh):
    placed = (
        P("col", "eb", None, None, None),
        P("col", "eb", None, None, None),
        P("col", "eb"),
        P(),
        P("col", None, None, None),
    )
    return jax.shard_map(
        body,
        mesh=mesh,
        in_specs=placed,
        out_specs=P("eb", "col", None, None, None, None),
        check_vma=False,
    )
```

```python
import functools
import math

import jax
import jax.numpy as jnp
import numpy as np
from jax import lax
from jax.experimental import pallas as pl
from jax.experimental.pallas import tpu as pltpu
from jax.sharding import PartitionSpec as P

f32 = jnp.float32
bf16 = jnp.bfloat16
LANES = 128


def halves(x):
    high = x.astype(bf16)
    low = (x - high.astype(f32)).astype(bf16)
    return high, low


def product(a, b):
    (ah, al), (bh, bl) = a, b
    dot = lambda u, v: jnp.dot(u, v, preferred_element_type=f32)
    return dot(ah, bh) + (dot(ah, bl) + dot(al, bh))


def transform_tables(n_energy):
    k = np.arange(n_energy)
    angle = np.pi * (2 * k[:, None] + 1) * k[None, :] / (2 * n_energy)
    c, s = np.cos(angle), np.sin(angle)
    forward = np.concatenate([c, s], axis=0)
    scale = 2.0 / (2 * n_energy * math.sqrt(n_energy))
    backward = np.concatenate([c.T, -s.T], axis=1) * scale
    return forward.astype(np.float32), backward.astype(np.float32)


def numpy_halves(x):
    high = x.astype(bf16)
    low = (x - high.astype(np.float32)).astype(bf16)
    return high, low


def correlate_kernel(
    slots, sizes, n_energy, n_dest,
    emap_hbm, forward_hbm, back_hbm, less_hbm, more_hbm,
    out_hbm, emap_ref, forward_ref, back_ref, less_ref, more_ref, back,
    small_sem, less_sem, more_sem, out_sem, *buffers,
):
    small = [
        pltpu.make_async_copy(source, target, small_sem.at[i])
        for i, (source, target) in enumerate(
            (
                (emap_hbm, emap_ref), (back_hbm, back_ref), (forward_hbm, forward_ref),
            )
        )
    ]

    def slot_copies(slot):
        return (
            pltpu.make_async_copy(less_hbm.at[slot], less_ref.at[slot], less_sem.at[slot]),
            pltpu.make_async_copy(more_hbm.at[slot], more_ref.at[slot], more_sem.at[slot]),
        )

    for copy in small:
        copy.start()
    for slot in range(slots):
        for copy in slot_copies(slot):
            copy.start()
    for copy in small:
        copy.wait()
    row = jnp.broadcast_to(emap_ref[...], (n_dest, n_energy))
    i0 = lax.broadcasted_iota(jnp.int32, (n_dest, n_energy), 0)
    i1 = lax.broadcasted_iota(jnp.int32, (n_dest, n_energy), 1)
    column = jnp.sum(jnp.where(i0 == i1, row, 0), axis=1, keepdims=True)
    pick = jnp.where(i1 == column, 1.0, 0.0).astype(bf16)
    for part in range(2):
        back[part * n_dest:(part + 1) * n_dest, :] = jnp.dot(
            pick,
            back_ref[part * n_energy:(part + 1) * n_energy, :],
            preferred_element_type=f32,
        ).astype(bf16)

    def pieces(ref, first, size):
        read = lambda slot, q: ref[slot, pl.ds(q, n_energy, stride=4), :]
        return jnp.concatenate(
            [read(first + i, q) for qs in ((0, 2), (1, 3)) for i in range(size) for q in qs],
            axis=1,
        )

    def spectrum(ref, first, size):
        high, low = halves(pieces(ref, first, size))
        value = jnp.dot(
            forward_ref[...],
            jnp.concatenate([high, high, low], axis=0),
            preferred_element_type=f32,
        )
        half = value.shape[1] // 2
        return (
            value[:n_energy, :half], value[:n_energy, half:],
            value[n_energy:, :half], value[n_energy:, half:],
        )

    def batch(first, size, buffer):
        a, c, d, b = spectrum(less_ref, first, size)
        e, g, h, f = spectrum(more_ref, first, size)
        sum_re = a * e + b * f + c * g + d * h
        dif_re = a * f + b * e - c * h - d * g
        sum_im = c * e - d * f - a * g + b * h
        dif_im = c * f - d * e + a * h - b * g
        pairs = jnp.concatenate(
            [
                jnp.concatenate([sum_im, -dif_re], axis=0),
                jnp.concatenate([-sum_re, -dif_im], axis=0),
            ],
            axis=1,
        )
        high, low = halves(pairs)
        series = jnp.dot(
            back[...], jnp.concatenate([high, low], axis=0), preferred_element_type=f32
        )
        series = series[:n_dest] + series[n_dest:]
        for i in range(size):
            for q in range(4):
                at = ((q // 2) * 2 * size + 2 * i + q % 2) * LANES
                buffer[pl.ds(i * 4 + q, n_dest, stride=size * 4), :] = series[
                    :, at:at + LANES
                ]

    first, sends = 0, []
    for part, size in enumerate(sizes):
        for slot in range(first, first + size):
            for copy in slot_copies(slot):
                copy.wait()
        batch(first, size, buffers[part])
        send = pltpu.make_async_copy(
            buffers[part].reshape(n_dest, size * 4, LANES),
            out_hbm.at[:, pl.ds(first * 4, size * 4), :],
            out_sem.at[part],
        )
        send.start()
        sends.append(send)
        first += size
    for send in sends:
        send.wait()


def correlate(less, more, emap, n_dest, interpret=False):
    slots, n_energy = less.shape[0], less.shape[1]
    sizes = (6, 6)
    forward, backward = transform_tables(n_energy)
    high, low = numpy_halves(forward)
    table = np.concatenate([high, low, high], axis=1)
    high, low = numpy_halves(backward)
    back = np.block([[high, high], [low, np.zeros_like(low)]])

    def packed(x):
        x = x.reshape(slots, n_energy, 2, 2, LANES).transpose(0, 1, 3, 2, 4)
        return x.reshape(slots, n_energy * 4, LANES)

    kernel = lambda *refs: correlate_kernel(
        slots, sizes, n_energy, n_dest, *refs
    )
    hbm = pl.BlockSpec(memory_space=pltpu.HBM)
    rows = (slots, n_energy * 4, LANES)
    return pl.pallas_call(
        kernel,
        in_specs=[hbm] * 5,
        out_specs=hbm,
        out_shape=jax.ShapeDtypeStruct((n_dest, slots * 4, LANES), f32),
        scratch_shapes=[
            pltpu.VMEM((1, n_energy), jnp.int32),
            pltpu.VMEM(table.shape, bf16),
            pltpu.VMEM(back.shape, bf16),
            pltpu.VMEM(rows, f32),
            pltpu.VMEM(rows, f32),
            pltpu.VMEM((2 * n_dest, 4 * n_energy), bf16),
            pltpu.SemaphoreType.DMA((3,)),
            pltpu.SemaphoreType.DMA((slots,)),
            pltpu.SemaphoreType.DMA((slots,)),
            pltpu.SemaphoreType.DMA((len(sizes),)),
        ] + [pltpu.VMEM((n_dest * size * 4, LANES), f32) for size in sizes],
        compiler_params=pltpu.CompilerParams(vmem_limit_bytes=32 << 20),
        interpret=interpret,
    )(*[
        pltpu.with_memory_space_constraint(x, pltpu.HBM)
        for x in (emap.reshape(1, n_energy), jnp.asarray(table), jnp.asarray(back),
                  packed(less), packed(more))
    ])


def placed(block, slots, n_source, order, group, in_ref, by_slot):
    stride = slots * 4
    total = None
    for g in range(0, slots, group):
        row = jnp.concatenate([by_slot[s:s + 1, :] for s in range(g, g + group)], axis=1)
        tile = lax.broadcasted_iota(jnp.int32, (order, group * n_source), 0) + block * order
        pick = jnp.where(tile == row, 1.0, 0.0).astype(bf16)
        values = jnp.concatenate(
            [
                jnp.concatenate(
                    [in_ref[pl.ds(s * 4 + q, n_source, stride=stride), :] for q in range(4)],
                    axis=1,
                )
                for s in range(g, g + group)
            ],
            axis=0,
        )
        parts = [jnp.dot(pick, x, preferred_element_type=f32) for x in halves(values)]
        total = parts if total is None else [t + x for t, x in zip(total, parts)]
    return total[0] + total[1]


def joined(x, axis):
    return jnp.concatenate([x[0], x[1]], axis=axis)


def right(parts, weight):
    rows = jnp.concatenate([joined(x, 0) for x in parts], axis=0)
    value = product(halves(rows), weight)
    n = parts[0].shape[1]
    pieces = [value[i * n:(i + 1) * n] for i in range(2 * len(parts))]
    return [
        jnp.concatenate(pieces[2 * i:2 * i + 2], axis=1) for i in range(len(parts))
    ]


def stacked(weights):
    return jnp.concatenate(halves(jnp.concatenate(weights, axis=0)), axis=0)


def times(weights, high, low):
    rows = weights.shape[0] // 2
    dot = lambda u, v: jnp.dot(u, v, preferred_element_type=f32)
    first = dot(weights, high)
    return first[:rows] + (first[rows:] + dot(weights[:rows], low))


def left(weights, value):
    total = times(stacked(weights), *halves(value))
    n = weights[0].shape[0]
    return [total[i * n:(i + 1) * n] for i in range(len(weights))]


def upper(lower):
    return jnp.stack([-jnp.transpose(lower[0]), jnp.transpose(lower[1])])


def store(ref, value):
    n = ref.shape[-1]
    ref[0, :, :] = value[:, :n]
    ref[1, :, :] = value[:, n:]


def first_kernel(rows, in_ref, ids_ref, lower_ref):
    store(lower_ref, placed(1, *rows, in_ref, ids_ref))


def local_kernel(
    rows, in_ref, ids_ref, lower_ref, v_prev, v_here, up_ref, down_ref, middle_ref, below_ref
):
    order = lower_ref.shape[-1]
    diag = placed(0, *rows, in_ref, ids_ref)
    diag = jnp.stack([diag[:, :order], diag[:, order:]])
    lower = lower_ref[...]
    vd, vl = v_here[0], v_here[1]
    vl_half = halves(vl)
    (for_up,) = right([diag], halves(jnp.transpose(vl)))
    (for_up,) = left([vl], for_up)
    store(up_ref, for_up)
    (for_down,) = right([diag], halves(v_prev[1]))
    store(down_ref, for_down)
    middle, below = right([diag, lower], halves(jnp.transpose(vd)))
    (from_upper,) = right([upper(lower)], vl_half)
    middle_ref[...] = middle + from_upper
    below_ref[...] = below


def lower_kernel(
    prev_ref, next_ref, middle_ref, v_prev, v_here, v_next,
    diag_ref, lower_ref, diag_w, lower_w,
):
    diag_w[...] = stacked([jnp.transpose(v_here[1])])
    lower_w[...] = stacked([v_next[0]])
    prev = prev_ref[...]
    vl_prev, vd, vl, vl_next = v_prev[1], v_here[0], v_here[1], v_next[1]
    (above,) = right([upper(prev)], halves(jnp.transpose(vd)))
    (middle,) = right([prev], halves(jnp.transpose(vl_prev)))
    (farther,) = right([next_ref[...]], halves(vl))
    diag, lower = left([vd, vl], middle + middle_ref[...])
    diag_ref[...] = diag + left([vl_prev], above)[0]
    lower_ref[...] = lower + left([jnp.transpose(vl_next)], farther)[0]


def last_kernel(
    prev_ref, next_ref, below_ref, diag_ref, lower_ref, diag_w, lower_w,
    out_hbm, buffer, sems,
):
    high, low = halves(below_ref[...] + joined(next_ref[...], 1))
    copies = [pltpu.make_async_copy(buffer.at[k], out_hbm.at[k], sems.at[k]) for k in range(2)]
    diag = times(diag_w[...], high, low)
    store(buffer.at[0], diag + (diag_ref[...] + joined(prev_ref[...], 1)))
    copies[0].start()
    store(buffer.at[1], times(lower_w[...], high, low) + lower_ref[...])
    copies[1].start()
    for copy in copies:
        copy.wait()


def block_call(kernel, outs, products, interpret, *args, **options):
    shapes = [
        out if isinstance(out, jax.ShapeDtypeStruct) else jax.ShapeDtypeStruct(out, f32)
        for out in outs
    ]
    order = args[-1].shape[-1]
    return pl.pallas_call(
        kernel,
        out_shape=shapes,
        **options,
        compiler_params=pltpu.CompilerParams(vmem_limit_bytes=32 << 20),
        cost_estimate=pl.CostEstimate(
            flops=products * 3 * 4 * order**3,
            bytes_accessed=sum(4 * math.prod(x.shape) for x in (*args, *shapes)),
            transcendentals=0,
        ),
        interpret=interpret,
    )(*args)


def shifted(value, axis, step):
    devices = lax.axis_size(axis)
    return lax.ppermute(value, axis, [(i, (i + step) % devices) for i in range(devices)])


def screen(arrived, ids, slots, n_source, v_prev, v_here, v_next, shift, interpret=False):
    b = v_here.shape[-1]
    block, wide = (2, b, b), (b, 2 * b)
    rows = (slots, n_source, b, 4)
    (lower,) = block_call(
        functools.partial(first_kernel, rows), (block,), 2, interpret, arrived, ids
    )
    lower_prev, lower_next = shift(lower, 1), shift(lower, -1)
    for_up, for_down, middle, below = block_call(
        functools.partial(local_kernel, rows), (block, block, wide, wide), 8, interpret,
        arrived, ids, lower, v_prev, v_here,
    )
    diag_prev, diag_next = shift(for_up, 1), shift(for_down, -1)
    weights = jax.ShapeDtypeStruct((2 * b, b), bf16)
    diag_part, lower_part, diag_w, lower_w = block_call(
        lower_kernel, (wide, wide, weights, weights), 7, interpret,
        lower_prev, lower_next, middle, v_prev, v_here, v_next,
    )
    (result,) = block_call(
        last_kernel, ((2, 2, b, b),), 2, interpret,
        diag_prev, diag_next, below, diag_part, lower_part, diag_w, lower_w,
        out_specs=[pl.BlockSpec(memory_space=pltpu.HBM)],
        scratch_shapes=[pltpu.VMEM((2, 2, b, b), f32), pltpu.SemaphoreType.DMA((2,))],
    )
    return result


def tiles_held(tiles, n_eb):
    inner = 16
    along_z = [[y * inner + z for z in range(inner)] for y in range(n_eb // inner)]
    along_y = [[y * inner + z for y in range(n_eb // inner)] for z in range(inner)]
    for groups in (along_z, along_y):
        tiles = lax.all_gather(tiles, "eb", axis=0, tiled=True, axis_index_groups=groups)
    return tiles.T


def body(g_lesser, g_greater, owner_tiles, energy_map, coulomb):
    slots = g_lesser.shape[1]
    n_eb = lax.axis_size("eb")
    shift = lambda value, step: shifted(value, "col", step)
    v_here = coulomb[0]
    sent = correlate(g_lesser[0], g_greater[0], energy_map, n_eb)
    sent, v_moved, tiles_moved = lax.optimization_barrier((sent, v_here, owner_tiles))
    v_prev, v_next = shift(v_moved, 1), shift(v_moved, -1)
    arrived = lax.all_to_all(sent, "eb", split_axis=0, concat_axis=0, tiled=True)
    ids = tiles_held(tiles_moved, n_eb)
    arrived, ids, v_prev, v_next = lax.optimization_barrier((arrived, ids, v_prev, v_next))
    arrived = arrived.reshape(-1, LANES)
    return screen(arrived, ids, slots, n_eb, v_prev, v_here, v_next, shift)[None, None]


def solution(mesh):
    placed = (
        P("col", "eb", None, None, None),
        P("col", "eb", None, None, None),
        P("col", "eb"),
        P(),
        P("col", None, None, None),
    )
    return jax.shard_map(
        body,
        mesh=mesh,
        in_specs=placed,
        out_specs=P("eb", "col", None, None, None, None),
        check_vma=False,
    )
```

```python
import functools
import math

import jax
import jax.numpy as jnp
import numpy as np
from jax import lax
from jax.experimental import pallas as pl
from jax.experimental.pallas import tpu as pltpu
from jax.sharding import PartitionSpec as P

f32 = jnp.float32
bf16 = jnp.bfloat16
LANES = 128


def halves(x):
    high = x.astype(bf16)
    low = (x - high.astype(f32)).astype(bf16)
    return high, low


def product(a, b):
    (ah, al), (bh, bl) = a, b
    dot = lambda u, v: jnp.dot(u, v, preferred_element_type=f32)
    return dot(ah, bh) + (dot(ah, bl) + dot(al, bh))


def transform_tables(n_energy):
    k = np.arange(n_energy)
    angle = np.pi * (2 * k[:, None] + 1) * k[None, :] / (2 * n_energy)
    c, s = np.cos(angle), np.sin(angle)
    forward = np.concatenate([c, s], axis=0)
    scale = 2.0 / (2 * n_energy * math.sqrt(n_energy))
    backward = np.concatenate([c.T, -s.T], axis=1) * scale
    return forward.astype(np.float32), backward.astype(np.float32)


def numpy_halves(x):
    high = x.astype(bf16)
    low = (x - high.astype(np.float32)).astype(bf16)
    return high, low


def correlate_kernel(
    slots, sizes, n_energy, n_dest, stride,
    tiles_hbm, emap_hbm, forward_hbm, back_hbm, less_hbm, more_hbm,
    out_ref, tiles_ref, emap_ref, forward_ref, back_ref, less_ref, more_ref, back,
    small_sem, less_sem, more_sem,
):
    small = [
        pltpu.make_async_copy(source, target, small_sem.at[i])
        for i, (source, target) in enumerate(
            (
                (tiles_hbm, tiles_ref), (emap_hbm, emap_ref),
                (back_hbm, back_ref), (forward_hbm, forward_ref),
            )
        )
    ]

    def slot_copies(slot):
        return (
            pltpu.make_async_copy(less_hbm.at[slot], less_ref.at[slot], less_sem.at[slot]),
            pltpu.make_async_copy(more_hbm.at[slot], more_ref.at[slot], more_sem.at[slot]),
        )

    for copy in small:
        copy.start()
    for slot in range(slots):
        for copy in slot_copies(slot):
            copy.start()
    for copy in small:
        copy.wait()
    lane = lax.broadcasted_iota(jnp.int32, (1, LANES), 1)
    ids = jnp.zeros((1, LANES), jnp.int32)
    for slot in range(slots):
        ids = jnp.where(lane == slot, tiles_ref[0, slot], ids)
    out_ref[pl.ds(stride - 1, n_dest, stride=stride), :] = jnp.broadcast_to(
        ids.astype(f32), (n_dest, LANES)
    )
    row = jnp.broadcast_to(emap_ref[...], (n_dest, n_energy))
    i0 = lax.broadcasted_iota(jnp.int32, (n_dest, n_energy), 0)
    i1 = lax.broadcasted_iota(jnp.int32, (n_dest, n_energy), 1)
    column = jnp.sum(jnp.where(i0 == i1, row, 0), axis=1, keepdims=True)
    pick = jnp.where(i1 == column, 1.0, 0.0).astype(bf16)
    for part in range(2):
        back[part * n_dest:(part + 1) * n_dest, :] = jnp.dot(
            pick,
            back_ref[part * n_energy:(part + 1) * n_energy, :],
            preferred_element_type=f32,
        ).astype(bf16)

    def pieces(ref, first, size):
        read = lambda slot, q: ref[slot, pl.ds(q, n_energy, stride=4), :]
        return jnp.concatenate(
            [read(first + i, q) for qs in ((0, 2), (1, 3)) for i in range(size) for q in qs],
            axis=1,
        )

    def spectrum(ref, first, size):
        high, low = halves(pieces(ref, first, size))
        value = jnp.dot(
            forward_ref[...],
            jnp.concatenate([high, high, low], axis=0),
            preferred_element_type=f32,
        )
        half = value.shape[1] // 2
        return (
            value[:n_energy, :half], value[:n_energy, half:],
            value[n_energy:, :half], value[n_energy:, half:],
        )

    def batch(first, size):
        a, c, d, b = spectrum(less_ref, first, size)
        e, g, h, f = spectrum(more_ref, first, size)
        sum_re = a * e + b * f + c * g + d * h
        dif_re = a * f + b * e - c * h - d * g
        sum_im = c * e - d * f - a * g + b * h
        dif_im = c * f - d * e + a * h - b * g
        pairs = jnp.concatenate(
            [
                jnp.concatenate([sum_im, -dif_re], axis=0),
                jnp.concatenate([-sum_re, -dif_im], axis=0),
            ],
            axis=1,
        )
        high, low = halves(pairs)
        series = jnp.dot(
            back[...], jnp.concatenate([high, low], axis=0), preferred_element_type=f32
        )
        series = series[:n_dest] + series[n_dest:]
        for i in range(size):
            for q in range(4):
                at = ((q // 2) * 2 * size + 2 * i + q % 2) * LANES
                out_ref[pl.ds((first + i) * 4 + q, n_dest, stride=stride), :] = series[
                    :, at:at + LANES
                ]

    first = 0
    for size in sizes:
        for slot in range(first, first + size):
            for copy in slot_copies(slot):
                copy.wait()
        batch(first, size)
        first += size


def correlate(less, more, tiles, emap, n_dest, interpret=False):
    slots, n_energy = less.shape[0], less.shape[1]
    stride = slots * 4 + 1
    sizes = (4, 8)
    forward, backward = transform_tables(n_energy)
    high, low = numpy_halves(forward)
    table = np.concatenate([high, low, high], axis=1)
    high, low = numpy_halves(backward)
    back = np.block([[high, high], [low, np.zeros_like(low)]])

    def packed(x):
        x = x.reshape(slots, n_energy, 2, 2, LANES).transpose(0, 1, 3, 2, 4)
        return x.reshape(slots, n_energy * 4, LANES)

    kernel = lambda *refs: correlate_kernel(
        slots, sizes, n_energy, n_dest, stride, *refs
    )
    hbm = pl.BlockSpec(memory_space=pltpu.HBM)
    rows = (slots, n_energy * 4, LANES)
    return pl.pallas_call(
        kernel,
        in_specs=[hbm] * 6,
        out_specs=pl.BlockSpec(memory_space=pltpu.VMEM),
        out_shape=jax.ShapeDtypeStruct((n_dest * stride, LANES), f32),
        scratch_shapes=[
            pltpu.SMEM((1, slots), jnp.int32),
            pltpu.VMEM((1, n_energy), jnp.int32),
            pltpu.VMEM(table.shape, bf16),
            pltpu.VMEM(back.shape, bf16),
            pltpu.VMEM(rows, f32),
            pltpu.VMEM(rows, f32),
            pltpu.VMEM((2 * n_dest, 4 * n_energy), bf16),
            pltpu.SemaphoreType.DMA((4,)),
            pltpu.SemaphoreType.DMA((slots,)),
            pltpu.SemaphoreType.DMA((slots,)),
        ],
        compiler_params=pltpu.CompilerParams(vmem_limit_bytes=32 << 20),
        interpret=interpret,
    )(*[
        pltpu.with_memory_space_constraint(x, pltpu.HBM)
        for x in (tiles, emap.reshape(1, n_energy), jnp.asarray(table), jnp.asarray(back),
                  packed(less), packed(more))
    ])


def placed(block, slots, n_source, order, group, in_ref):
    stride = slots * 4 + 1
    ids = in_ref[pl.ds(stride - 1, n_source, stride=stride), :]
    by_slot = jnp.transpose(ids)
    total = None
    for g in range(0, slots, group):
        row = jnp.concatenate([by_slot[s:s + 1, :] for s in range(g, g + group)], axis=1)
        tile = lax.broadcasted_iota(jnp.int32, (order, group * n_source), 0) + block * order
        pick = jnp.where(tile.astype(f32) == row, 1.0, 0.0).astype(bf16)
        values = jnp.concatenate(
            [
                jnp.concatenate(
                    [in_ref[pl.ds(s * 4 + q, n_source, stride=stride), :] for q in range(4)],
                    axis=1,
                )
                for s in range(g, g + group)
            ],
            axis=0,
        )
        parts = [jnp.dot(pick, x, preferred_element_type=f32) for x in halves(values)]
        total = parts if total is None else [t + x for t, x in zip(total, parts)]
    return total[0] + total[1]


def joined(x, axis):
    return jnp.concatenate([x[0], x[1]], axis=axis)


def right(parts, weight):
    rows = jnp.concatenate([joined(x, 0) for x in parts], axis=0)
    value = product(halves(rows), weight)
    n = parts[0].shape[1]
    pieces = [value[i * n:(i + 1) * n] for i in range(2 * len(parts))]
    return [
        jnp.concatenate(pieces[2 * i:2 * i + 2], axis=1) for i in range(len(parts))
    ]


def stacked(weights):
    return jnp.concatenate(halves(jnp.concatenate(weights, axis=0)), axis=0)


def times(weights, high, low):
    rows = weights.shape[0] // 2
    dot = lambda u, v: jnp.dot(u, v, preferred_element_type=f32)
    first = dot(weights, high)
    return first[:rows] + (first[rows:] + dot(weights[:rows], low))


def left(weights, value):
    total = times(stacked(weights), *halves(value))
    n = weights[0].shape[0]
    return [total[i * n:(i + 1) * n] for i in range(len(weights))]


def upper(lower):
    return jnp.stack([-jnp.transpose(lower[0]), jnp.transpose(lower[1])])


def store(ref, value):
    n = ref.shape[-1]
    ref[0, :, :] = value[:, :n]
    ref[1, :, :] = value[:, n:]


def first_kernel(rows, in_ref, lower_ref):
    store(lower_ref, placed(1, *rows, in_ref))


def own_parity():
    return lax.rem(lax.axis_index("col"), 2) == 0


def choose(even, x, y):
    return jnp.where(even, x, y)


def diagonal_kernel(rows, in_ref, v_prev, v_here, diag_ref, outer_ref, inner_ref):
    order = v_here.shape[-1]
    diag = placed(0, *rows, in_ref)
    store(diag_ref, diag)
    diag = jnp.stack([diag[:, :order], diag[:, order:]])
    vl = v_here[1]
    (for_up,) = right([diag], halves(jnp.transpose(vl)))
    (for_up,) = left([vl], for_up)
    (for_down,) = right([diag], halves(v_prev[1]))
    even = own_parity()
    store(outer_ref, choose(even, for_down, for_up))
    store(inner_ref, choose(even, for_up, for_down))


def local_kernel(diag_ref, lower_ref, v_here, middle_ref, below_ref):
    lower = lower_ref[...]
    middle, below = right([diag_ref[...], lower], halves(jnp.transpose(v_here[0])))
    (from_upper,) = right([upper(lower)], halves(v_here[1]))
    middle_ref[...] = middle + from_upper
    below_ref[...] = below


def lower_kernel(
    outer_ref, inner_ref, middle_ref, v_prev, v_here, v_next,
    diag_ref, lower_ref, diag_w, lower_w,
):
    diag_w[...] = stacked([jnp.transpose(v_here[1])])
    lower_w[...] = stacked([v_next[0]])
    even = own_parity()
    outer, inner = outer_ref[...], inner_ref[...]
    prev, following = choose(even, outer, inner), choose(even, inner, outer)
    vl_prev, vd, vl, vl_next = v_prev[1], v_here[0], v_here[1], v_next[1]
    (above,) = right([upper(prev)], halves(jnp.transpose(vd)))
    (middle,) = right([prev], halves(jnp.transpose(vl_prev)))
    (farther,) = right([following], halves(vl))
    diag, lower = left([vd, vl], middle + middle_ref[...])
    diag_ref[...] = diag + left([vl_prev], above)[0]
    lower_ref[...] = lower + left([jnp.transpose(vl_next)], farther)[0]


def last_kernel(
    outer_ref, inner_ref, below_ref, diag_ref, lower_ref, diag_w, lower_w,
    out_hbm, buffer, sems,
):
    even = own_parity()
    outer, inner = joined(outer_ref[...], 1), joined(inner_ref[...], 1)
    high, low = halves(below_ref[...] + choose(even, inner, outer))
    copies = [pltpu.make_async_copy(buffer.at[k], out_hbm.at[k], sems.at[k]) for k in range(2)]
    diag = times(diag_w[...], high, low)
    store(buffer.at[0], diag + (diag_ref[...] + choose(even, outer, inner)))
    copies[0].start()
    store(buffer.at[1], times(lower_w[...], high, low) + lower_ref[...])
    copies[1].start()
    for copy in copies:
        copy.wait()


def block_call(kernel, outs, products, interpret, *args, **options):
    shapes = [
        out if isinstance(out, jax.ShapeDtypeStruct) else jax.ShapeDtypeStruct(out, f32)
        for out in outs
    ]
    order = args[-1].shape[-1]
    return pl.pallas_call(
        kernel,
        out_shape=shapes,
        **options,
        compiler_params=pltpu.CompilerParams(vmem_limit_bytes=32 << 20),
        cost_estimate=pl.CostEstimate(
            flops=products * 3 * 4 * order**3,
            bytes_accessed=sum(4 * math.prod(x.shape) for x in (*args, *shapes)),
            transcendentals=0,
        ),
        interpret=interpret,
    )(*args)


def shifted(value, axis, step):
    devices = lax.axis_size(axis)
    return lax.ppermute(value, axis, [(i, (i + step) % devices) for i in range(devices)])


def across(value, axis, even_step):
    devices = lax.axis_size(axis)
    step = lambda i: even_step if i % 2 == 0 else -even_step
    return lax.ppermute(value, axis, [(i, (i + step(i)) % devices) for i in range(devices)])


def screen(arrived, slots, n_source, v_prev, v_here, v_next, interpret=False):
    b = v_here.shape[-1]
    block, wide = (2, b, b), (b, 2 * b)
    rows = (slots, n_source, b, 4)
    outer, inner = (lambda x: across(x, "col", -1)), (lambda x: across(x, "col", 1))
    (lower,) = block_call(
        functools.partial(first_kernel, rows), (block,), 2, interpret, arrived
    )
    lower_outer, lower_inner = outer(lower), inner(lower)
    diag, for_outer, for_inner = block_call(
        functools.partial(diagonal_kernel, rows), (block,) * 3, 5, interpret,
        arrived, v_prev, v_here,
    )
    diag_outer, diag_inner = outer(for_outer), inner(for_inner)
    middle, below = block_call(
        local_kernel, (wide, wide), 3, interpret, diag, lower, v_here
    )
    weights = jax.ShapeDtypeStruct((2 * b, b), bf16)
    diag_part, lower_part, diag_w, lower_w = block_call(
        lower_kernel, (wide, wide, weights, weights), 7, interpret,
        lower_outer, lower_inner, middle, v_prev, v_here, v_next,
    )
    (result,) = block_call(
        last_kernel, ((2, 2, b, b),), 2, interpret,
        diag_outer, diag_inner, below, diag_part, lower_part, diag_w, lower_w,
        out_specs=[pl.BlockSpec(memory_space=pltpu.HBM)],
        scratch_shapes=[pltpu.VMEM((2, 2, b, b), f32), pltpu.SemaphoreType.DMA((2,))],
    )
    return result


def body(g_lesser, g_greater, owner_tiles, energy_map, coulomb):
    slots = g_lesser.shape[1]
    n_eb = lax.axis_size("eb")
    shift = lambda value, step: shifted(value, "col", step)
    v_here = coulomb[0]
    sent = correlate(g_lesser[0], g_greater[0], owner_tiles, energy_map, n_eb)
    sent, v_moved = lax.optimization_barrier((sent, v_here))
    v_prev, v_next = shift(v_moved, 1), shift(v_moved, -1)
    arrived = lax.all_to_all(
        sent.reshape(n_eb, 1, -1), "eb", split_axis=0, concat_axis=0, tiled=True
    )
    arrived, v_prev, v_next = lax.optimization_barrier((arrived, v_prev, v_next))
    arrived = arrived.reshape(-1, LANES)
    return screen(arrived, slots, n_eb, v_prev, v_here, v_next)[None, None]


def solution(mesh):
    placed = (
        P("col", "eb", None, None, None),
        P("col", "eb", None, None, None),
        P("col", "eb"),
        P(),
        P("col", None, None, None),
    )
    return jax.shard_map(
        body,
        mesh=mesh,
        in_specs=placed,
        out_specs=P("eb", "col", None, None, None, None),
        check_vma=False,
    )
```

```python
import functools
import math

import jax
import jax.numpy as jnp
import numpy as np
from jax import lax
from jax.experimental import pallas as pl
from jax.experimental.pallas import tpu as pltpu
from jax.sharding import PartitionSpec as P

f32 = jnp.float32
bf16 = jnp.bfloat16
LANES = 128


def halves(x):
    high = x.astype(bf16)
    low = (x - high.astype(f32)).astype(bf16)
    return high, low


def product(a, b):
    (ah, al), (bh, bl) = a, b
    dot = lambda u, v: jnp.dot(u, v, preferred_element_type=f32)
    return dot(ah, bh) + (dot(ah, bl) + dot(al, bh))


def transform_tables(n_energy):
    k = np.arange(n_energy)
    angle = np.pi * (2 * k[:, None] + 1) * k[None, :] / (2 * n_energy)
    c, s = np.cos(angle), np.sin(angle)
    forward = np.concatenate([c, s], axis=0)
    scale = 2.0 / (2 * n_energy * math.sqrt(n_energy))
    backward = np.concatenate([c.T, -s.T], axis=1) * scale
    return forward.astype(np.float32), backward.astype(np.float32)


def numpy_halves(x):
    high = x.astype(bf16)
    low = (x - high.astype(np.float32)).astype(bf16)
    return high, low


def correlate_kernel(
    slots, sizes, n_energy, n_dest, stride,
    tiles_hbm, emap_hbm, forward_hbm, back_hbm, less_hbm, more_hbm,
    out_ref, tiles_ref, emap_ref, forward_ref, back_ref, less_ref, more_ref, back,
    small_sem, less_sem, more_sem,
):
    small = [
        pltpu.make_async_copy(source, target, small_sem.at[i])
        for i, (source, target) in enumerate(
            (
                (tiles_hbm, tiles_ref), (emap_hbm, emap_ref),
                (back_hbm, back_ref), (forward_hbm, forward_ref),
            )
        )
    ]

    def slot_copies(slot):
        return (
            pltpu.make_async_copy(less_hbm.at[slot], less_ref.at[slot], less_sem.at[slot]),
            pltpu.make_async_copy(more_hbm.at[slot], more_ref.at[slot], more_sem.at[slot]),
        )

    for copy in small:
        copy.start()
    for slot in range(slots):
        for copy in slot_copies(slot):
            copy.start()
    for copy in small:
        copy.wait()
    lane = lax.broadcasted_iota(jnp.int32, (1, LANES), 1)
    ids = jnp.zeros((1, LANES), jnp.int32)
    for slot in range(slots):
        ids = jnp.where(lane == slot, tiles_ref[0, slot], ids)
    out_ref[pl.ds(stride - 1, n_dest, stride=stride), :] = jnp.broadcast_to(
        ids.astype(f32), (n_dest, LANES)
    )
    row = jnp.broadcast_to(emap_ref[...], (n_dest, n_energy))
    i0 = lax.broadcasted_iota(jnp.int32, (n_dest, n_energy), 0)
    i1 = lax.broadcasted_iota(jnp.int32, (n_dest, n_energy), 1)
    column = jnp.sum(jnp.where(i0 == i1, row, 0), axis=1, keepdims=True)
    pick = jnp.where(i1 == column, 1.0, 0.0).astype(bf16)
    for part in range(2):
        back[part * n_dest:(part + 1) * n_dest, :] = jnp.dot(
            pick,
            back_ref[part * n_energy:(part + 1) * n_energy, :],
            preferred_element_type=f32,
        ).astype(bf16)

    def pieces(ref, first, size):
        read = lambda slot, q: ref[slot, pl.ds(q, n_energy, stride=4), :]
        return jnp.concatenate(
            [read(first + i, q) for qs in ((0, 2), (1, 3)) for i in range(size) for q in qs],
            axis=1,
        )

    def spectrum(ref, first, size):
        high, low = halves(pieces(ref, first, size))
        value = jnp.dot(
            forward_ref[...],
            jnp.concatenate([high, high, low], axis=0),
            preferred_element_type=f32,
        )
        half = value.shape[1] // 2
        return (
            value[:n_energy, :half], value[:n_energy, half:],
            value[n_energy:, :half], value[n_energy:, half:],
        )

    def batch(first, size):
        a, c, d, b = spectrum(less_ref, first, size)
        e, g, h, f = spectrum(more_ref, first, size)
        sum_re = a * e + b * f + c * g + d * h
        dif_re = a * f + b * e - c * h - d * g
        sum_im = c * e - d * f - a * g + b * h
        dif_im = c * f - d * e + a * h - b * g
        pairs = jnp.concatenate(
            [
                jnp.concatenate([sum_im, -dif_re], axis=0),
                jnp.concatenate([-sum_re, -dif_im], axis=0),
            ],
            axis=1,
        )
        high, low = halves(pairs)
        series = jnp.dot(
            back[...], jnp.concatenate([high, low], axis=0), preferred_element_type=f32
        )
        series = series[:n_dest] + series[n_dest:]
        for i in range(size):
            for q in range(4):
                at = ((q // 2) * 2 * size + 2 * i + q % 2) * LANES
                out_ref[pl.ds((first + i) * 4 + q, n_dest, stride=stride), :] = series[
                    :, at:at + LANES
                ]

    first = 0
    for size in sizes:
        for slot in range(first, first + size):
            for copy in slot_copies(slot):
                copy.wait()
        batch(first, size)
        first += size


def correlate(less, more, tiles, emap, n_dest, interpret=False):
    slots, n_energy = less.shape[0], less.shape[1]
    stride = slots * 4 + 1
    sizes = (4, 8)
    forward, backward = transform_tables(n_energy)
    high, low = numpy_halves(forward)
    table = np.concatenate([high, low, high], axis=1)
    high, low = numpy_halves(backward)
    back = np.block([[high, high], [low, np.zeros_like(low)]])

    def packed(x):
        x = x.reshape(slots, n_energy, 2, 2, LANES).transpose(0, 1, 3, 2, 4)
        return x.reshape(slots, n_energy * 4, LANES)

    kernel = lambda *refs: correlate_kernel(
        slots, sizes, n_energy, n_dest, stride, *refs
    )
    hbm = pl.BlockSpec(memory_space=pltpu.HBM)
    rows = (slots, n_energy * 4, LANES)
    return pl.pallas_call(
        kernel,
        in_specs=[hbm] * 6,
        out_specs=pl.BlockSpec(memory_space=pltpu.VMEM),
        out_shape=jax.ShapeDtypeStruct((n_dest * stride, LANES), f32),
        scratch_shapes=[
            pltpu.SMEM((1, slots), jnp.int32),
            pltpu.VMEM((1, n_energy), jnp.int32),
            pltpu.VMEM(table.shape, bf16),
            pltpu.VMEM(back.shape, bf16),
            pltpu.VMEM(rows, f32),
            pltpu.VMEM(rows, f32),
            pltpu.VMEM((2 * n_dest, 4 * n_energy), bf16),
            pltpu.SemaphoreType.DMA((4,)),
            pltpu.SemaphoreType.DMA((slots,)),
            pltpu.SemaphoreType.DMA((slots,)),
        ],
        compiler_params=pltpu.CompilerParams(vmem_limit_bytes=32 << 20),
        interpret=interpret,
    )(*[
        pltpu.with_memory_space_constraint(x, pltpu.HBM)
        for x in (tiles, emap.reshape(1, n_energy), jnp.asarray(table), jnp.asarray(back),
                  packed(less), packed(more))
    ])


def placed(block, slots, n_source, order, group, in_ref):
    stride = slots * 4 + 1
    ids = in_ref[pl.ds(stride - 1, n_source, stride=stride), :]
    by_slot = jnp.transpose(ids)
    total = None
    for g in range(0, slots, group):
        row = jnp.concatenate([by_slot[s:s + 1, :] for s in range(g, g + group)], axis=1)
        tile = lax.broadcasted_iota(jnp.int32, (order, group * n_source), 0) + block * order
        pick = jnp.where(tile.astype(f32) == row, 1.0, 0.0).astype(bf16)
        values = jnp.concatenate(
            [
                jnp.concatenate(
                    [in_ref[pl.ds(s * 4 + q, n_source, stride=stride), :] for q in range(4)],
                    axis=1,
                )
                for s in range(g, g + group)
            ],
            axis=0,
        )
        parts = [jnp.dot(pick, x, preferred_element_type=f32) for x in halves(values)]
        total = parts if total is None else [t + x for t, x in zip(total, parts)]
    return total[0] + total[1]


def joined(x, axis):
    return jnp.concatenate([x[0], x[1]], axis=axis)


def right(parts, weight):
    rows = jnp.concatenate([joined(x, 0) for x in parts], axis=0)
    value = product(halves(rows), weight)
    n = parts[0].shape[1]
    pieces = [value[i * n:(i + 1) * n] for i in range(2 * len(parts))]
    return [
        jnp.concatenate(pieces[2 * i:2 * i + 2], axis=1) for i in range(len(parts))
    ]


def stacked(weights):
    return jnp.concatenate(halves(jnp.concatenate(weights, axis=0)), axis=0)


def times(weights, high, low):
    rows = weights.shape[0] // 2
    dot = lambda u, v: jnp.dot(u, v, preferred_element_type=f32)
    first = dot(weights, high)
    return first[:rows] + (first[rows:] + dot(weights[:rows], low))


def left(weights, value):
    total = times(stacked(weights), *halves(value))
    n = weights[0].shape[0]
    return [total[i * n:(i + 1) * n] for i in range(len(weights))]


def upper(lower):
    return jnp.stack([-jnp.transpose(lower[0]), jnp.transpose(lower[1])])


def store(ref, value):
    n = ref.shape[-1]
    ref[0, :, :] = value[:, :n]
    ref[1, :, :] = value[:, n:]


def first_kernel(rows, in_ref, lower_ref):
    store(lower_ref, placed(1, *rows, in_ref))


def diagonal_kernel(rows, in_ref, v_prev, v_here, diag_ref, up_ref, down_ref):
    order = v_here.shape[-1]
    diag = placed(0, *rows, in_ref)
    store(diag_ref, diag)
    diag = jnp.stack([diag[:, :order], diag[:, order:]])
    vl = v_here[1]
    (for_up,) = right([diag], halves(jnp.transpose(vl)))
    (for_up,) = left([vl], for_up)
    store(up_ref, for_up)
    (for_down,) = right([diag], halves(v_prev[1]))
    store(down_ref, for_down)


def local_kernel(diag_ref, lower_ref, v_here, middle_ref, below_ref):
    lower = lower_ref[...]
    middle, below = right([diag_ref[...], lower], halves(jnp.transpose(v_here[0])))
    (from_upper,) = right([upper(lower)], halves(v_here[1]))
    middle_ref[...] = middle + from_upper
    below_ref[...] = below


def lower_kernel(
    prev_ref, next_ref, middle_ref, v_prev, v_here, v_next,
    diag_ref, lower_ref, diag_w, lower_w,
):
    diag_w[...] = stacked([jnp.transpose(v_here[1])])
    lower_w[...] = stacked([v_next[0]])
    prev = prev_ref[...]
    vl_prev, vd, vl, vl_next = v_prev[1], v_here[0], v_here[1], v_next[1]
    (above,) = right([upper(prev)], halves(jnp.transpose(vd)))
    (middle,) = right([prev], halves(jnp.transpose(vl_prev)))
    (farther,) = right([next_ref[...]], halves(vl))
    diag, lower = left([vd, vl], middle + middle_ref[...])
    diag_ref[...] = diag + left([vl_prev], above)[0]
    lower_ref[...] = lower + left([jnp.transpose(vl_next)], farther)[0]


def last_kernel(
    prev_ref, next_ref, below_ref, diag_ref, lower_ref, diag_w, lower_w,
    out_hbm, buffer, sems,
):
    high, low = halves(below_ref[...] + joined(next_ref[...], 1))
    copies = [pltpu.make_async_copy(buffer.at[k], out_hbm.at[k], sems.at[k]) for k in range(2)]
    diag = times(diag_w[...], high, low)
    store(buffer.at[0], diag + (diag_ref[...] + joined(prev_ref[...], 1)))
    copies[0].start()
    store(buffer.at[1], times(lower_w[...], high, low) + lower_ref[...])
    copies[1].start()
    for copy in copies:
        copy.wait()


def block_call(kernel, outs, products, interpret, *args, **options):
    shapes = [
        out if isinstance(out, jax.ShapeDtypeStruct) else jax.ShapeDtypeStruct(out, f32)
        for out in outs
    ]
    order = args[-1].shape[-1]
    return pl.pallas_call(
        kernel,
        out_shape=shapes,
        **options,
        compiler_params=pltpu.CompilerParams(vmem_limit_bytes=32 << 20),
        cost_estimate=pl.CostEstimate(
            flops=products * 3 * 4 * order**3,
            bytes_accessed=sum(4 * math.prod(x.shape) for x in (*args, *shapes)),
            transcendentals=0,
        ),
        interpret=interpret,
    )(*args)


def shifted(value, axis, step):
    devices = lax.axis_size(axis)
    return lax.ppermute(value, axis, [(i, (i + step) % devices) for i in range(devices)])


def screen(arrived, slots, n_source, v_prev, v_here, v_next, shift, interpret=False):
    b = v_here.shape[-1]
    block, wide = (2, b, b), (b, 2 * b)
    rows = (slots, n_source, b, 4)
    (lower,) = block_call(
        functools.partial(first_kernel, rows), (block,), 2, interpret, arrived
    )
    lower_prev, lower_next = shift(lower, 1), shift(lower, -1)
    diag, for_up, for_down = block_call(
        functools.partial(diagonal_kernel, rows), (block,) * 3, 5, interpret,
        arrived, v_prev, v_here,
    )
    diag_prev, diag_next = shift(for_up, 1), shift(for_down, -1)
    middle, below = block_call(
        local_kernel, (wide, wide), 3, interpret, diag, lower, v_here
    )
    weights = jax.ShapeDtypeStruct((2 * b, b), bf16)
    diag_part, lower_part, diag_w, lower_w = block_call(
        lower_kernel, (wide, wide, weights, weights), 7, interpret,
        lower_prev, lower_next, middle, v_prev, v_here, v_next,
    )
    (result,) = block_call(
        last_kernel, ((2, 2, b, b),), 2, interpret,
        diag_prev, diag_next, below, diag_part, lower_part, diag_w, lower_w,
        out_specs=[pl.BlockSpec(memory_space=pltpu.HBM)],
        scratch_shapes=[pltpu.VMEM((2, 2, b, b), f32), pltpu.SemaphoreType.DMA((2,))],
    )
    return result


def body(g_lesser, g_greater, owner_tiles, energy_map, coulomb):
    slots = g_lesser.shape[1]
    n_eb = lax.axis_size("eb")
    shift = lambda value, step: shifted(value, "col", step)
    v_here = coulomb[0]
    sent = correlate(g_lesser[0], g_greater[0], owner_tiles, energy_map, n_eb)
    sent, v_moved = lax.optimization_barrier((sent, v_here))
    v_prev, v_next = shift(v_moved, 1), shift(v_moved, -1)
    arrived = lax.all_to_all(
        sent.reshape(n_eb, 1, -1), "eb", split_axis=0, concat_axis=0, tiled=True
    )
    arrived, v_prev, v_next = lax.optimization_barrier((arrived, v_prev, v_next))
    arrived = arrived.reshape(-1, LANES)
    return screen(arrived, slots, n_eb, v_prev, v_here, v_next, shift)[None, None]


def solution(mesh):
    placed = (
        P("col", "eb", None, None, None),
        P("col", "eb", None, None, None),
        P("col", "eb"),
        P(),
        P("col", None, None, None),
    )
    return jax.shard_map(
        body,
        mesh=mesh,
        in_specs=placed,
        out_specs=P("eb", "col", None, None, None, None),
        check_vma=False,
    )
```

```python
import functools
import math

import jax
import jax.numpy as jnp
import numpy as np
from jax import lax
from jax.experimental import pallas as pl
from jax.experimental.pallas import tpu as pltpu
from jax.sharding import PartitionSpec as P

f32 = jnp.float32
bf16 = jnp.bfloat16
LANES = 128


def halves(x):
    high = x.astype(bf16)
    low = (x - high.astype(f32)).astype(bf16)
    return high, low


def product(a, b):
    (ah, al), (bh, bl) = a, b
    dot = lambda u, v: jnp.dot(u, v, preferred_element_type=f32)
    return dot(ah, bh) + (dot(ah, bl) + dot(al, bh))


def transform_tables(n_energy):
    k = np.arange(n_energy)
    angle = np.pi * (2 * k[:, None] + 1) * k[None, :] / (2 * n_energy)
    c, s = np.cos(angle), np.sin(angle)
    forward = np.concatenate([c, s], axis=0)
    scale = 2.0 / (2 * n_energy * math.sqrt(n_energy))
    backward = np.concatenate([c.T, -s.T], axis=1) * scale
    return forward.astype(np.float32), backward.astype(np.float32)


def numpy_halves(x):
    high = x.astype(bf16)
    low = (x - high.astype(np.float32)).astype(bf16)
    return high, low


def correlate_kernel(
    slots, sizes, n_energy, n_dest, stride,
    tiles_hbm, emap_hbm, forward_hbm, back_hbm, less_hbm, more_hbm,
    out_ref, tiles_ref, emap_ref, forward_ref, back_ref, less_ref, more_ref, back,
    small_sem, less_sem, more_sem,
):
    small = [
        pltpu.make_async_copy(source, target, small_sem.at[i])
        for i, (source, target) in enumerate(
            (
                (tiles_hbm, tiles_ref), (emap_hbm, emap_ref),
                (back_hbm, back_ref), (forward_hbm, forward_ref),
            )
        )
    ]

    def batch_copies(part):
        slots_of = pl.ds(sum(sizes[:part]), sizes[part])
        return (
            pltpu.make_async_copy(less_hbm.at[slots_of], less_ref.at[slots_of], less_sem.at[part]),
            pltpu.make_async_copy(more_hbm.at[slots_of], more_ref.at[slots_of], more_sem.at[part]),
        )

    for copy in small:
        copy.start()
    for part in range(len(sizes)):
        for copy in batch_copies(part):
            copy.start()
    for copy in small:
        copy.wait()
    lane = lax.broadcasted_iota(jnp.int32, (1, LANES), 1)
    ids = jnp.zeros((1, LANES), jnp.int32)
    for slot in range(slots):
        ids = jnp.where(lane == slot, tiles_ref[0, slot], ids)
    out_ref[pl.ds(stride - 1, n_dest, stride=stride), :] = jnp.broadcast_to(
        ids.astype(f32), (n_dest, LANES)
    )
    row = jnp.broadcast_to(emap_ref[...], (n_dest, n_energy))
    i0 = lax.broadcasted_iota(jnp.int32, (n_dest, n_energy), 0)
    i1 = lax.broadcasted_iota(jnp.int32, (n_dest, n_energy), 1)
    column = jnp.sum(jnp.where(i0 == i1, row, 0), axis=1, keepdims=True)
    pick = jnp.where(i1 == column, 1.0, 0.0).astype(bf16)
    for part in range(2):
        back[part * n_dest:(part + 1) * n_dest, :] = jnp.dot(
            pick,
            back_ref[part * n_energy:(part + 1) * n_energy, :],
            preferred_element_type=f32,
        ).astype(bf16)

    def pieces(ref, first, size):
        read = lambda slot, q: ref[slot, pl.ds(q, n_energy, stride=4), :]
        return jnp.concatenate(
            [read(first + i, q) for qs in ((0, 2), (1, 3)) for i in range(size) for q in qs],
            axis=1,
        )

    def spectrum(ref, first, size):
        high, low = halves(pieces(ref, first, size))
        value = jnp.dot(
            forward_ref[...],
            jnp.concatenate([high, high, low], axis=0),
            preferred_element_type=f32,
        )
        half = value.shape[1] // 2
        return (
            value[:n_energy, :half], value[:n_energy, half:],
            value[n_energy:, :half], value[n_energy:, half:],
        )

    def batch(first, size):
        a, c, d, b = spectrum(less_ref, first, size)
        e, g, h, f = spectrum(more_ref, first, size)
        sum_re = a * e + b * f + c * g + d * h
        dif_re = a * f + b * e - c * h - d * g
        sum_im = c * e - d * f - a * g + b * h
        dif_im = c * f - d * e + a * h - b * g
        pairs = jnp.concatenate(
            [
                jnp.concatenate([sum_im, -dif_re], axis=0),
                jnp.concatenate([-sum_re, -dif_im], axis=0),
            ],
            axis=1,
        )
        high, low = halves(pairs)
        series = jnp.dot(
            back[...], jnp.concatenate([high, low], axis=0), preferred_element_type=f32
        )
        series = series[:n_dest] + series[n_dest:]
        for i in range(size):
            for q in range(4):
                at = ((q // 2) * 2 * size + 2 * i + q % 2) * LANES
                out_ref[pl.ds((first + i) * 4 + q, n_dest, stride=stride), :] = series[
                    :, at:at + LANES
                ]

    first = 0
    for part, size in enumerate(sizes):
        for copy in batch_copies(part):
            copy.wait()
        batch(first, size)
        first += size


def correlate(less, more, tiles, emap, n_dest, interpret=False):
    slots, n_energy = less.shape[0], less.shape[1]
    stride = slots * 4 + 1
    sizes = (slots // 4, slots - slots // 4)
    forward, backward = transform_tables(n_energy)
    high, low = numpy_halves(forward)
    table = np.concatenate([high, low, high], axis=1)
    high, low = numpy_halves(backward)
    back = np.block([[high, high], [low, np.zeros_like(low)]])

    def packed(x):
        x = x.reshape(slots, n_energy, 2, 2, LANES).transpose(0, 1, 3, 2, 4)
        return x.reshape(slots, n_energy * 4, LANES)

    kernel = lambda *refs: correlate_kernel(
        slots, sizes, n_energy, n_dest, stride, *refs
    )
    hbm = pl.BlockSpec(memory_space=pltpu.HBM)
    rows = (slots, n_energy * 4, LANES)
    return pl.pallas_call(
        kernel,
        in_specs=[hbm] * 6,
        out_specs=pl.BlockSpec(memory_space=pltpu.VMEM),
        out_shape=jax.ShapeDtypeStruct((n_dest * stride, LANES), f32),
        scratch_shapes=[
            pltpu.SMEM((1, slots), jnp.int32),
            pltpu.VMEM((1, n_energy), jnp.int32),
            pltpu.VMEM(table.shape, bf16),
            pltpu.VMEM(back.shape, bf16),
            pltpu.VMEM(rows, f32),
            pltpu.VMEM(rows, f32),
            pltpu.VMEM((2 * n_dest, 4 * n_energy), bf16),
            pltpu.SemaphoreType.DMA((4,)),
            pltpu.SemaphoreType.DMA((len(sizes),)),
            pltpu.SemaphoreType.DMA((len(sizes),)),
        ],
        compiler_params=pltpu.CompilerParams(vmem_limit_bytes=32 << 20),
        interpret=interpret,
    )(*[
        pltpu.with_memory_space_constraint(x, pltpu.HBM)
        for x in (tiles, emap.reshape(1, n_energy), jnp.asarray(table), jnp.asarray(back),
                  packed(less), packed(more))
    ])


def placed(block, slots, n_source, order, group, in_ref):
    stride = slots * 4 + 1
    ids = in_ref[pl.ds(stride - 1, n_source, stride=stride), :]
    by_slot = jnp.transpose(ids)
    total = None
    for g in range(0, slots, group):
        row = jnp.concatenate([by_slot[s:s + 1, :] for s in range(g, g + group)], axis=1)
        tile = lax.broadcasted_iota(jnp.int32, (order, group * n_source), 0) + block * order
        pick = jnp.where(tile.astype(f32) == row, 1.0, 0.0).astype(bf16)
        values = jnp.concatenate(
            [
                jnp.concatenate(
                    [in_ref[pl.ds(s * 4 + q, n_source, stride=stride), :] for q in range(4)],
                    axis=1,
                )
                for s in range(g, g + group)
            ],
            axis=0,
        )
        parts = [jnp.dot(pick, x, preferred_element_type=f32) for x in halves(values)]
        total = parts if total is None else [t + x for t, x in zip(total, parts)]
    return total[0] + total[1]


def joined(x, axis):
    return jnp.concatenate([x[0], x[1]], axis=axis)


def right(parts, weight):
    rows = jnp.concatenate([joined(x, 0) for x in parts], axis=0)
    value = product(halves(rows), weight)
    n = parts[0].shape[1]
    pieces = [value[i * n:(i + 1) * n] for i in range(2 * len(parts))]
    return [
        jnp.concatenate(pieces[2 * i:2 * i + 2], axis=1) for i in range(len(parts))
    ]


def stacked(weights):
    return jnp.concatenate(halves(jnp.concatenate(weights, axis=0)), axis=0)


def times(weights, high, low):
    rows = weights.shape[0] // 2
    dot = lambda u, v: jnp.dot(u, v, preferred_element_type=f32)
    first = dot(weights, high)
    return first[:rows] + (first[rows:] + dot(weights[:rows], low))


def left(weights, value):
    total = times(stacked(weights), *halves(value))
    n = weights[0].shape[0]
    return [total[i * n:(i + 1) * n] for i in range(len(weights))]


def upper(lower):
    return jnp.stack([-jnp.transpose(lower[0]), jnp.transpose(lower[1])])


def store(ref, value):
    n = ref.shape[-1]
    ref[0, :, :] = value[:, :n]
    ref[1, :, :] = value[:, n:]


def first_kernel(rows, in_ref, lower_ref):
    store(lower_ref, placed(1, *rows, in_ref))


def local_kernel(
    rows, in_ref, lower_ref, v_prev, v_here, up_ref, down_ref, middle_ref, below_ref
):
    order = lower_ref.shape[-1]
    diag = placed(0, *rows, in_ref)
    diag = jnp.stack([diag[:, :order], diag[:, order:]])
    lower = lower_ref[...]
    vd, vl = v_here[0], v_here[1]
    vl_half = halves(vl)
    (for_up,) = right([diag], halves(jnp.transpose(vl)))
    (for_up,) = left([vl], for_up)
    store(up_ref, for_up)
    (for_down,) = right([diag], halves(v_prev[1]))
    store(down_ref, for_down)
    middle, below = right([diag, lower], halves(jnp.transpose(vd)))
    (from_upper,) = right([upper(lower)], vl_half)
    middle_ref[...] = middle + from_upper
    below_ref[...] = below


def lower_kernel(
    prev_ref, next_ref, middle_ref, v_prev, v_here, v_next,
    diag_ref, lower_ref, diag_w, lower_w,
):
    diag_w[...] = stacked([jnp.transpose(v_here[1])])
    lower_w[...] = stacked([v_next[0]])
    prev = prev_ref[...]
    vl_prev, vd, vl, vl_next = v_prev[1], v_here[0], v_here[1], v_next[1]
    (above,) = right([upper(prev)], halves(jnp.transpose(vd)))
    (middle,) = right([prev], halves(jnp.transpose(vl_prev)))
    (farther,) = right([next_ref[...]], halves(vl))
    diag, lower = left([vd, vl], middle + middle_ref[...])
    diag_ref[...] = diag + left([vl_prev], above)[0]
    lower_ref[...] = lower + left([jnp.transpose(vl_next)], farther)[0]


def last_kernel(
    prev_ref, next_ref, below_ref, diag_ref, lower_ref, diag_w, lower_w,
    out_hbm, buffer, sems,
):
    high, low = halves(below_ref[...] + joined(next_ref[...], 1))
    copies = [pltpu.make_async_copy(buffer.at[k], out_hbm.at[k], sems.at[k]) for k in range(2)]
    diag = times(diag_w[...], high, low)
    store(buffer.at[0], diag + (diag_ref[...] + joined(prev_ref[...], 1)))
    copies[0].start()
    store(buffer.at[1], times(lower_w[...], high, low) + lower_ref[...])
    copies[1].start()
    for copy in copies:
        copy.wait()


def block_call(kernel, outs, products, interpret, *args, **options):
    shapes = [
        out if isinstance(out, jax.ShapeDtypeStruct) else jax.ShapeDtypeStruct(out, f32)
        for out in outs
    ]
    order = args[-1].shape[-1]
    return pl.pallas_call(
        kernel,
        out_shape=shapes,
        **options,
        compiler_params=pltpu.CompilerParams(vmem_limit_bytes=32 << 20),
        cost_estimate=pl.CostEstimate(
            flops=products * 3 * 4 * order**3,
            bytes_accessed=sum(4 * math.prod(x.shape) for x in (*args, *shapes)),
            transcendentals=0,
        ),
        interpret=interpret,
    )(*args)


def shifted(value, axis, step):
    devices = lax.axis_size(axis)
    return lax.ppermute(value, axis, [(i, (i + step) % devices) for i in range(devices)])


def screen(arrived, slots, n_source, v_prev, v_here, v_next, shift, interpret=False):
    b = v_here.shape[-1]
    block, wide = (2, b, b), (b, 2 * b)
    rows = (slots, n_source, b, 4)
    (lower,) = block_call(
        functools.partial(first_kernel, rows), (block,), 2, interpret, arrived
    )
    lower_prev, lower_next = shift(lower, 1), shift(lower, -1)
    for_up, for_down, middle, below = block_call(
        functools.partial(local_kernel, rows), (block, block, wide, wide), 8, interpret,
        arrived, lower, v_prev, v_here,
    )
    diag_prev, diag_next = shift(for_up, 1), shift(for_down, -1)
    weights = jax.ShapeDtypeStruct((2 * b, b), bf16)
    diag_part, lower_part, diag_w, lower_w = block_call(
        lower_kernel, (wide, wide, weights, weights), 7, interpret,
        lower_prev, lower_next, middle, v_prev, v_here, v_next,
    )
    (result,) = block_call(
        last_kernel, ((2, 2, b, b),), 2, interpret,
        diag_prev, diag_next, below, diag_part, lower_part, diag_w, lower_w,
        out_specs=[pl.BlockSpec(memory_space=pltpu.HBM)],
        scratch_shapes=[pltpu.VMEM((2, 2, b, b), f32), pltpu.SemaphoreType.DMA((2,))],
    )
    return result


def body(g_lesser, g_greater, owner_tiles, energy_map, coulomb):
    slots = g_lesser.shape[1]
    n_eb = lax.axis_size("eb")
    shift = lambda value, step: shifted(value, "col", step)
    v_here = coulomb[0]
    sent = correlate(g_lesser[0], g_greater[0], owner_tiles, energy_map, n_eb)
    sent, v_moved = lax.optimization_barrier((sent, v_here))
    v_prev, v_next = shift(v_moved, 1), shift(v_moved, -1)
    arrived = lax.all_to_all(
        sent.reshape(n_eb, 1, -1), "eb", split_axis=0, concat_axis=0, tiled=True
    )
    arrived, v_prev, v_next = lax.optimization_barrier((arrived, v_prev, v_next))
    arrived = arrived.reshape(-1, LANES)
    return screen(arrived, slots, n_eb, v_prev, v_here, v_next, shift)[None, None]


def solution(mesh):
    placed = (
        P("col", "eb", None, None, None),
        P("col", "eb", None, None, None),
        P("col", "eb"),
        P(),
        P("col", None, None, None),
    )
    return jax.shard_map(
        body,
        mesh=mesh,
        in_specs=placed,
        out_specs=P("eb", "col", None, None, None, None),
        check_vma=False,
    )
```
